512 devices in a mesh: row: 16 (over y, core), col: 32 (over x, z).
Axes of the slice: x: 4, y: 8, z: 8, core: 2. Of those that a mesh axis runs over, the one named last changes fastest.
Arguments:
- operator_blocks: float32 [4096, 64, 512], P(('row', 'col')), may hold values from -0.75 to 0.75
- operator_count: int32 [4096], P(('row', 'col')), may hold values from 1 to 8
- operator_slot: int32 [4096, 8], P(('row', 'col')), may hold values from 0 to 127
- fetch_lists: int32 [16, 32, 32, 4], P('row', 'col'), may hold values from 0 to 4095, as said below
- prolong_blocks: float32 [4096, 64, 128], P(('row', 'col')), may hold values from -0.75 to 0.75
- prolong_cols: int32 [4096, 2], P(('row', 'col')), may hold values from 0 to 31
- restrict_blocks: float32 [4096, 64, 128], P(('row', 'col')), may hold values from -0.09375 to 0.09375
- restrict_rows: int32 [4096, 2], P(('row', 'col')), may hold values from 0 to 1
Outputs:
- coarse_operator: float32 [2048, 2048], P('row', 'col')
The draws below stay inside these ranges and needn't reach their ends.
Inputs may be any that keep to these rules, and one draw needn't show every extreme that they name: fetch_lists[r, c, p, s] names a fine block held by the device with column index p and row index r2 = (r + c + p * 4 + s + h) mod 16, for one whole number h of the draw; that device holds fine blocks (r2 * 32 + p) * 8 to (r2 * 32 + p + 1) * 8 - 1.
All inputs are finite; a program needn't handle non-finite values.
Results may differ from the reference program's by a relative error of at most 0.0003.
Values sent between devices are 32-bit elements; how exact they have to be, the bound alone decides.
A program may use at most 64 MiB of HBM per device.

```python
import jax
import jax.numpy as jnp
from jax import lax

BS = 64
KA = 8
KP = 2
KR = 2
SLOT = 4
NCR = 2
FBD = 8
NF = 4096
NC = 32
N_ROW = 16
N_COL = 32


def draw_fetch_lists(key, part):
    first, second = jax.random.split(jax.random.fold_in(key, 11))
    turn = jax.random.randint(first, (), 0, N_ROW)
    row_idx = jnp.arange(N_ROW, dtype=jnp.int32)[:, None, None, None]
    col_idx = jnp.arange(N_COL, dtype=jnp.int32)[None, :, None, None]
    peer_idx = jnp.arange(N_COL, dtype=jnp.int32)[None, None, :, None]
    slot_idx = jnp.arange(SLOT, dtype=jnp.int32)[None, None, None, :]
    owner_row = (row_idx + col_idx + peer_idx * SLOT + slot_idx + turn) % N_ROW
    inside = jax.random.randint(second, (N_ROW, N_COL, N_COL, SLOT), 0, FBD)
    holder = owner_row * N_COL + peer_idx
    inside = jnp.where(holder == 0, 0, inside)
    inside = jnp.where(holder == N_ROW * N_COL - 1, FBD - 1, inside)
    return (holder * FBD + inside).astype(jnp.int32)


def with_ends(values, stream_key, smallest, largest):
    shape = values.shape
    place = [jax.random.randint(jax.random.fold_in(stream_key, axis), (), 0, shape[axis]) for axis in range(len(shape))]
    values = values.at[tuple(place)].set(smallest)
    longest = shape.index(max(shape))
    place[longest] = (place[longest] + 1) % shape[longest]
    return values.at[tuple(place)].set(largest)


def steps_of(rng, dims, shards, smallest, largest):
    gain, own = 1.0, jax.random.fold_in(rng, 6)
    for position, parts in shards:
        heights = jnp.exp(jax.random.uniform(jax.random.fold_in(own, position), (parts,), jnp.float32, smallest / len(shards), largest / len(shards)))
        gain = gain * jnp.repeat(heights, dims[position] // parts).reshape([-1 if axis == position else 1 for axis in range(len(dims))])
    return gain


def centred(key, extent, scale, reach, cuts=(), kind=jnp.bfloat16):
    array = jax.random.normal(key, extent, jnp.float32) * scale
    if len(cuts) > 0:
        array = steps_of(key, extent, cuts, -0.22, 0.18) * array
    return jnp.clip(array, min=-reach, max=reach).astype(kind)


def setup_inputs(seed: int = 0) -> dict:
    streams_of = jax.random.split(jax.random.key(seed), 9)
    operator_blocks = centred(streams_of[0], (NF, BS, KA * BS), BS ** -0.5, 0.75, ((0, 512),), jnp.float32)
    operator_count = with_ends(jax.random.randint(streams_of[1], (NF,), 1, KA + 1), jax.random.fold_in(streams_of[1], 1), 1, KA).astype(jnp.int32)
    operator_slot = with_ends(jax.random.randint(streams_of[2], (NF, KA), 0, N_COL * SLOT), jax.random.fold_in(streams_of[2], 1), 0, (N_COL * SLOT) - 1).astype(jnp.int32)
    fetch_lists = draw_fetch_lists(jax.random.fold_in(streams_of[8], 71), 0)
    prolong_blocks = centred(streams_of[4], (NF, BS, KP * BS), BS ** -0.5, 0.75, ((0, 512),), jnp.float32)
    prolong_cols = with_ends(jax.random.randint(streams_of[5], (NF, KP), 0, NC), jax.random.fold_in(streams_of[5], 1), 0, NC - 1).astype(jnp.int32)
    restrict_blocks = centred(streams_of[6], (NF, BS, KR * BS), (BS * FBD * N_COL * KA * KP // NC // 2) ** -0.5, 0.09375, ((0, 512),), jnp.float32)
    restrict_rows = with_ends(jax.random.randint(streams_of[7], (NF, KR), 0, NCR), jax.random.fold_in(streams_of[7], 1), 0, NCR - 1).astype(jnp.int32)
    return dict(operator_blocks=operator_blocks, operator_count=operator_count, operator_slot=operator_slot, fetch_lists=fetch_lists, prolong_blocks=prolong_blocks, prolong_cols=prolong_cols, restrict_blocks=restrict_blocks, restrict_rows=restrict_rows)


def contract(form, left, right):
    return jnp.einsum(form, left, right, precision=lax.Precision.HIGHEST)


def reference(operator_blocks, operator_count, operator_slot, fetch_lists, prolong_blocks, prolong_cols, restrict_blocks, restrict_rows):
    slab_blocks = FBD * N_COL
    wanted_all = fetch_lists.reshape(N_ROW * N_COL, N_COL * SLOT)

    def mesh_slab(group):
        start = (group * slab_blocks).astype(jnp.int32)
        blocks = lax.dynamic_slice_in_dim(operator_blocks, start, slab_blocks, 0).reshape(slab_blocks, BS, KA, BS)
        counts = lax.dynamic_slice_in_dim(operator_count, start, slab_blocks, 0)
        slots = lax.dynamic_slice_in_dim(operator_slot, start, slab_blocks, 0)
        restrict_part = lax.dynamic_slice_in_dim(restrict_blocks, start, slab_blocks, 0).reshape(slab_blocks, BS, KR, BS)
        restrict_idx = lax.dynamic_slice_in_dim(restrict_rows, start, slab_blocks, 0)
        device = group * N_COL + jnp.arange(slab_blocks, dtype=jnp.int32) // FBD
        fine_index = wanted_all[device[:, None], slots]
        picked = prolong_blocks[fine_index]
        picked_columns = prolong_cols[fine_index]
        live_mask = (jnp.arange(KA, dtype=jnp.int32)[None, :] < counts[:, None]).astype(jnp.float32)
        products = contract("iakb,ikbn->ikan", blocks, picked)
        prolong_hot = (picked_columns[..., None] == jnp.arange(NC, dtype=jnp.int32)).astype(jnp.float32) * live_mask[:, :, None, None]
        product_dense = contract("ikamc,ikmJ->iaJc", products.reshape(slab_blocks, KA, BS, KP, BS), prolong_hot)
        restrict_hot = (restrict_idx[..., None] == jnp.arange(NCR, dtype=jnp.int32)).astype(jnp.float32)
        restrict_dense = contract("iaqb,iqQ->iaQb", restrict_part, restrict_hot)
        return contract("iaQb,iaJc->QbJc", restrict_dense, product_dense).reshape(NCR * BS, NC * BS)

    stacked = lax.map(mesh_slab, jnp.arange(N_ROW, dtype=jnp.int32))
    return stacked.reshape(NC * BS, NC * BS)
```

```python
import jax
import jax.numpy as jnp
from jax import lax
from jax.sharding import PartitionSpec as P

NCR = 2


def contract(form, left, right):
    return jnp.einsum(form, left, right, precision=lax.Precision.HIGHEST)


def gather_panel(prolong_blocks, prolong_cols):
    return (
        lax.all_gather(prolong_blocks, "row", axis=0, tiled=True),
        lax.all_gather(prolong_cols, "row", axis=0, tiled=True),
    )


def local(
    operator_blocks,
    operator_count,
    operator_slot,
    fetch_lists,
    prolong_blocks,
    prolong_cols,
    restrict_blocks,
    restrict_rows,
):
    fine_rows = operator_blocks.shape[0]
    block_size = operator_blocks.shape[1]
    row_entries = operator_slot.shape[1]
    prolong_entries = prolong_cols.shape[1]
    restrict_entries = restrict_rows.shape[1]
    columns = lax.axis_size("col")
    slot_count = fetch_lists.shape[3]
    total_slots = columns * slot_count
    coarse_all = NCR * lax.axis_size("row")
    live_mask = (
        jnp.arange(row_entries, dtype=jnp.int32)[None, :] < operator_count[:, None]
    ).astype(jnp.float32)
    blocks = operator_blocks.reshape(fine_rows, block_size, row_entries, block_size)
    restrict_hot = (restrict_rows[..., None] == jnp.arange(NCR, dtype=jnp.int32)).astype(
        jnp.float32
    )
    restrict_dense = contract(
        "iaqb,iqQ->iaQb",
        restrict_blocks.reshape(fine_rows, block_size, restrict_entries, block_size),
        restrict_hot,
    )
    requests = fetch_lists.reshape(columns, slot_count)
    panel_blocks, panel_columns = gather_panel(prolong_blocks, prolong_cols)
    wanted = lax.all_to_all(requests, "col", split_axis=0, concat_axis=0, tiled=True)
    position = wanted // (fine_rows * columns) * fine_rows + wanted % fine_rows
    fetched = panel_blocks[position]
    fetched_columns = panel_columns[position]
    got_blocks = lax.all_to_all(fetched, "col", split_axis=0, concat_axis=0, tiled=True)
    got_columns = lax.all_to_all(fetched_columns, "col", split_axis=0, concat_axis=0, tiled=True)
    got_blocks = got_blocks.reshape(total_slots, block_size, prolong_entries * block_size)
    got_columns = got_columns.reshape(total_slots, prolong_entries)
    picked = got_blocks[operator_slot]
    picked_columns = got_columns[operator_slot]
    products = contract("iakb,ikbn->ikan", blocks, picked)
    prolong_hot = (picked_columns[..., None] == jnp.arange(coarse_all, dtype=jnp.int32)).astype(
        jnp.float32
    ) * live_mask[:, :, None, None]
    product_dense = contract(
        "ikamc,ikmJ->iaJc",
        products.reshape(fine_rows, row_entries, block_size, prolong_entries, block_size),
        prolong_hot,
    )
    partial_value = contract("iaQb,iaJc->JcQb", restrict_dense, product_dense)
    partial_value = partial_value.reshape(coarse_all, block_size, NCR * block_size)
    shares = lax.all_to_all(partial_value, "col", split_axis=0, concat_axis=0, tiled=True)
    return shares.sum(axis=0).T


def solution(mesh):
    return jax.shard_map(
        local,
        mesh=mesh,
        in_specs=(
            P(("row", "col"), None, None),
            P(("row", "col")),
            P(("row", "col"), None),
            P("row", "col", None, None),
            P(("row", "col"), None, None),
            P(("row", "col"), None),
            P(("row", "col"), None, None),
            P(("row", "col"), None),
        ),
        out_specs=P("row", "col"),
        check_vma=False,
    )
```

```python
import functools

import jax
import jax.numpy as jnp
from jax import lax
from jax.experimental import pallas as pl
from jax.experimental.pallas import tpu as pltpu
from jax.sharding import PartitionSpec as P

MESH = pl.DeviceIdType.MESH
F32 = jnp.float32
BF16 = jnp.bfloat16

NX, NZ = 4, 8
CORES = 2
NCR = 2
FBD = 8
SLOT = 4
BS = 64
HALF = BS // 2


class Geometry:
    def __init__(self, rows, cols, x=NX, z=NZ, slot=SLOT):
        self.rows, self.cols, self.x, self.z, self.slot = rows, cols, x, z, slot
        self.y = rows // CORES
        self.pair = z * slot // rows
        self.out_y = slot * HALF + 8
        self.out_z = self.pair * (BS - HALF)


def half_ring(n):
    return n // 2, n - 1 - n // 2


def fetch_kernel(
    g, idxy_ref, idxz_ref, p_ref, tag_ref, gy_ref, gz_ref,
    pan_y, pan_z, pan_t, st_y, st_z, iy, iz, sy, sz,
    yu_s, yu_r, yd_s, yd_r, zu_s, zu_r, zd_s, zd_r, sib_s, sib_r,
    ix_s, ix_r, ex_s, ex_r, loc,
):
    me_r, me_c = lax.axis_index("row"), lax.axis_index("col")
    y, core = me_r // CORES, me_r % CORES
    x, z = me_c // g.z, me_c % g.z
    low = BS - HALF

    def peer_y(t, sign):
        dx, dz = t // g.z, t % g.z
        px = (x + sign * dx + g.x) % g.x
        pz = (z + sign * dz + g.z) % g.z
        return px * g.z + pz

    def peer_z(t, sign):
        dr, dx = t // g.x, t % g.x
        pr = (me_r + sign * dr + g.rows) % g.rows
        px = (x + sign * dx + g.x) % g.x
        return pr, px

    n_y, n_z = g.cols, g.rows * g.x
    barrier = pltpu.get_barrier_semaphore()

    @pl.loop(1, n_y)
    def _(t):
        pl.semaphore_signal(barrier, inc=1, device_id=(me_r, peer_y(t, 1)), device_id_type=MESH)

    @pl.loop(1, n_z)
    def _(t):
        pr, px = peer_z(t, 1)
        pl.semaphore_signal(barrier, inc=1, device_id=(pr, px * g.z + z), device_id_type=MESH)

    for j in range(FBD):
        pan_y[me_r * FBD + j] = p_ref[j, 0:HALF, :]
        pan_z[z * FBD + j] = p_ref[j, HALF:BS, :]
        pan_t[j] = tag_ref[j]
    iy[0] = idxy_ref[me_c]
    iz[0] = idxz_ref[me_r * g.x + x]

    pl.semaphore_wait(barrier, n_y - 1 + n_z - 1)

    def row_of(yy):
        return ((yy + g.y) % g.y) * CORES + core

    def ring_y(t, sign, send, recv):
        src = pan_y.at[pl.ds(row_of(y - sign * (t - 1)) * FBD, FBD)]
        dst_row = row_of(y + sign)
        return pltpu.make_async_remote_copy(
            src_ref=src, dst_ref=src, send_sem=send.at[t - 1], recv_sem=recv.at[t - 1],
            device_id=(dst_row, me_c), device_id_type=MESH,
        )

    def ring_z(t, sign, send, recv):
        at = (z - sign * (t - 1) + g.z) % g.z
        src = pan_z.at[pl.ds(at * FBD, FBD)]
        return pltpu.make_async_remote_copy(
            src_ref=src, dst_ref=src, send_sem=send.at[t - 1], recv_sem=recv.at[t - 1],
            device_id=(me_r, x * g.z + (z + sign + g.z) % g.z), device_id_type=MESH,
        )

    def sibling(yy, slot):
        src = pan_y.at[pl.ds(row_of(yy) * FBD, FBD)]
        return pltpu.make_async_remote_copy(
            src_ref=src, dst_ref=src, send_sem=sib_s.at[slot], recv_sem=sib_r.at[slot],
            device_id=(y * CORES + (1 - core), me_c), device_id_type=MESH,
        )

    up_y, down_y = half_ring(g.y)
    up_z, down_z = half_ring(g.z)
    rings = [
        (ring_y, 1, up_y, yu_s, yu_r), (ring_z, 1, up_z, zu_s, zu_r),
        (ring_y, -1, down_y, yd_s, yd_r), (ring_z, -1, down_z, zd_s, zd_r),
    ]
    for make, sign, steps, send, recv in rings:
        if steps:
            make(1, sign, send, recv).start()
    sibs = [sibling(y, 0)]
    sibs[0].start()

    @pl.loop(1, g.rows)
    def _(d):
        pltpu.make_async_remote_copy(
            src_ref=tag_ref, dst_ref=pan_t.at[pl.ds(d * FBD, FBD)], send_sem=ix_s.at[2], recv_sem=ix_r.at[2],
            device_id=((me_r - d + g.rows) % g.rows, me_c), device_id_type=MESH,
        ).start()

    @pl.loop(1, n_y)
    def _(t):
        dev = peer_y(t, -1)
        pltpu.make_async_remote_copy(
            src_ref=idxy_ref.at[dev], dst_ref=iy.at[t], send_sem=ix_s.at[0], recv_sem=ix_r.at[0],
            device_id=(me_r, dev), device_id_type=MESH,
        ).start()

    @pl.loop(1, n_z)
    def _(t):
        pr, px = peer_z(t, -1)
        pltpu.make_async_remote_copy(
            src_ref=idxz_ref.at[pr * g.x + px], dst_ref=iz.at[t], send_sem=ix_s.at[1], recv_sem=ix_r.at[1],
            device_id=(pr, px * g.z + z), device_id_type=MESH,
        ).start()

    for t in range(1, max(up_y, up_z) + 1):
        for make, sign, steps, send, recv in rings:
            if t <= steps:
                make(t, sign, send, recv).wait_recv()
                if t < steps:
                    make(t + 1, sign, send, recv).start()
                if make is ring_y:
                    copy = sibling(y - sign * t, len(sibs))
                    copy.start()
                    sibs.append(copy)

    def all_of(buf, count, send, recv, unit=1):
        view = buf.at[pl.ds(unit, (count - 1) * unit)]
        return pltpu.make_async_remote_copy(
            src_ref=view, dst_ref=view, send_sem=send, recv_sem=recv,
            device_id=(me_r, me_c), device_id_type=MESH,
        )

    all_of(iy, n_y, ix_s.at[0], ix_r.at[0]).wait_recv()
    all_of(iz, n_z, ix_s.at[1], ix_r.at[1]).wait_recv()
    all_of(pan_t, g.rows, ix_s.at[2], ix_r.at[2], FBD).wait_recv()
    to_sy = pltpu.make_async_copy(iy, sy, loc.at[0])
    to_sz = pltpu.make_async_copy(iz, sz, loc.at[1])
    to_sy.start()
    to_sz.start()
    to_sy.wait()
    to_sz.wait()
    for copy in sibs:
        copy.wait_recv()

    def stage_y(t):
        for s in range(g.slot):
            st_y[t, s * HALF:(s + 1) * HALF, :] = pan_y[sy[t, 0, s]]
            tag = pan_t[sy[t, 0, g.slot + s]]
            for rep in range(8 // g.slot):
                row = g.slot * HALF + rep * g.slot + s
                st_y[t, row:row + 1, :] = tag

    def stage_z(t):
        for s in range(g.pair):
            st_z[t, s * low:(s + 1) * low, :] = pan_z[sz[t, 0, s]]

    def send_y(q):
        t = (q * 13) % n_y
        stage_y(t)
        pltpu.make_async_remote_copy(
            src_ref=st_y.at[t], dst_ref=gy_ref.at[t], send_sem=ex_s.at[0], recv_sem=ex_r.at[0],
            device_id=(me_r, peer_y(t, 1)), device_id_type=MESH,
        ).start()

    def send_z(q):
        t = (q * 29) % n_z
        stage_z(t)
        pr, px = peer_z(t, 1)
        pltpu.make_async_remote_copy(
            src_ref=st_z.at[t], dst_ref=gz_ref.at[t], send_sem=ex_s.at[1], recv_sem=ex_r.at[1],
            device_id=(pr, px * g.z + z), device_id_type=MESH,
        ).start()

    ratio = n_z // n_y

    @pl.loop(1, n_y)
    def _(q):
        send_y(q)
        for j in range(ratio):
            send_z(ratio * q - j)

    for j in range(1, ratio):
        send_z(n_z - j)

    stage_y(0)
    stage_z(0)
    own_a = pltpu.make_async_copy(st_y.at[0], gy_ref.at[0], loc.at[2])
    own_b = pltpu.make_async_copy(st_z.at[0], gz_ref.at[0], loc.at[3])
    own_a.start()
    own_b.start()

    for make, sign, steps, send, recv in rings:
        for t in range(1, steps + 1):
            make(t, sign, send, recv).wait_send()
    for copy in sibs:
        copy.wait_send()
    all_of(iy, n_y, ix_s.at[0], ix_r.at[0]).wait_send()
    all_of(iz, n_z, ix_s.at[1], ix_r.at[1]).wait_send()
    all_of(pan_t, g.rows, ix_s.at[2], ix_r.at[2], FBD).wait_send()
    own_a.wait()
    own_b.wait()
    all_of(st_y, n_y, ex_s.at[0], ex_r.at[0]).wait_send()
    all_of(st_z, n_z, ex_s.at[1], ex_r.at[1]).wait_send()
    all_of(gy_ref, n_y, ex_s.at[0], ex_r.at[0]).wait_recv()
    all_of(gz_ref, n_z, ex_s.at[1], ex_r.at[1]).wait_recv()


def fetch(g, idxy, idxz, prolong_blocks, tags):
    up_y, down_y = half_ring(g.y)
    up_z, down_z = half_ring(g.z)
    dma = pltpu.SemaphoreType.DMA
    n_y, n_z = g.cols, g.rows * g.x
    vmem = pl.BlockSpec(memory_space=pltpu.VMEM)
    return pl.pallas_call(
        functools.partial(fetch_kernel, g),
        out_shape=(
            jax.ShapeDtypeStruct((n_y, g.out_y, 128), F32),
            jax.ShapeDtypeStruct((n_z, g.out_z, 128), F32),
        ),
        in_specs=[vmem] * 4,
        out_specs=(pl.BlockSpec(memory_space=pl.ANY),) * 2,
        scratch_shapes=[
            pltpu.VMEM((g.rows * FBD, HALF, 128), F32),
            pltpu.VMEM((g.z * FBD, BS - HALF, 128), F32),
            pltpu.VMEM((g.rows * FBD, 1, 128), F32),
            pltpu.VMEM((n_y, g.out_y, 128), F32),
            pltpu.VMEM((n_z, g.out_z, 128), F32),
            pltpu.VMEM((n_y, 1, 128), jnp.int32),
            pltpu.VMEM((n_z, 1, 128), jnp.int32),
            pltpu.SMEM((n_y, 1, 128), jnp.int32),
            pltpu.SMEM((n_z, 1, 128), jnp.int32),
            dma((up_y,)), dma((up_y,)), dma((max(down_y, 1),)), dma((max(down_y, 1),)),
            dma((up_z,)), dma((up_z,)), dma((max(down_z, 1),)), dma((max(down_z, 1),)),
            dma((g.y,)), dma((g.y,)),
            dma((3,)), dma((3,)), dma((2,)), dma((2,)), dma((4,)),
        ],
        compiler_params=pltpu.CompilerParams(
            collective_id=0, has_side_effects=True, vmem_limit_bytes=32 << 20
        ),
        name="fetch",
    )(idxy, idxz, prolong_blocks, tags)


def split(value):
    high = value.astype(BF16)
    return high, (value - high.astype(F32)).astype(BF16)


def dot_t(left, right):
    return lax.dot_general(left, right, (((0,), (0,)), ((), ())), preferred_element_type=F32)


def product_kernel(
    g, fetch_ref, slot_ref, count_ref, rows_ref, a_ref, r_ref, gy_hbm, gz_hbm, acc_ref,
    gy, gz, tags, w, sem,
):
    me_r, me_c = lax.axis_index("row"), lax.axis_index("col")
    x, z = me_c // g.z, me_c % g.z
    n_i, _, width = a_ref.shape
    n_k = width // BS
    low = BS - HALF
    copies = [
        pltpu.make_async_copy(gy_hbm, gy, sem.at[0]),
        pltpu.make_async_copy(gz_hbm, gz, sem.at[1]),
        pltpu.make_async_copy(gy_hbm.at[:, pl.ds(g.slot * HALF, 8), :], tags, sem.at[2]),
    ]
    for copy in copies:
        copy.start()
    acc_ref[...] = jnp.zeros_like(acc_ref)
    lane = lax.broadcasted_iota(jnp.int32, (BS, 2 * BS), 1) // BS

    @pl.loop(0, n_i)
    def _(i):
        stored = r_ref[i]
        swapped = pltpu.roll(stored, BS, 1)
        first, second = rows_ref[i, 0], rows_ref[i, 1]
        own = jnp.where(lane == 0, first, second)
        other = jnp.where(lane == 0, second, first)
        dense = jnp.where(own == lane, stored, 0.0) + jnp.where(other == lane, swapped, 0.0)
        r_hi, r_lo = split(dense)
        a_hi, a_lo = split(a_ref[i])
        ra = dot_t(
            jnp.concatenate([a_hi, a_lo, a_hi], axis=0),
            jnp.concatenate([r_hi, r_hi, r_lo], axis=0),
        )
        for k in range(n_k):
            part = jnp.where(k < count_ref[i], ra[k * BS:(k + 1) * BS, :], 0.0)
            hi, lo = split(part)
            at = i * n_k + k
            w[at, 0:BS, :] = hi
            w[at, BS:2 * BS, :] = hi
            w[at, 2 * BS:3 * BS, :] = lo

    for copy in copies:
        copy.wait()

    @pl.loop(0, n_i)
    def _(i):
        for k in range(n_k):
            slot = slot_ref[i, k]
            peer, s = slot // g.slot, slot % g.slot
            px, pz = peer // g.z, peer % g.z
            owner_row = fetch_ref[peer, s] // (FBD * g.cols)
            dx = (x - px + g.x) % g.x
            t = dx * g.z + (z - pz + g.z) % g.z
            tz = ((me_r - owner_row + g.rows) % g.rows) * g.x + dx
            j = pz // (g.z // g.pair)
            top = gy[t, pl.ds(pl.multiple_of(s * HALF, 8), HALF), :]
            bottom = gz[tz, pl.ds(pl.multiple_of(j * low, 8), low), :]
            p_hi, p_lo = split(jnp.concatenate([top, bottom], axis=0))
            out = dot_t(jnp.concatenate([p_hi, p_lo, p_hi], axis=0), w[i * n_k + k])
            first = tags[t, s, 0].astype(jnp.int32)
            second = tags[t, s, BS].astype(jnp.int32)
            acc_ref[first] += out[0:BS, :]
            acc_ref[second] += out[BS:2 * BS, :]


def product(g, requests, slots, counts, rows, blocks, restrict, gy, gz):
    n_i, _, width = blocks.shape
    n_k = width // BS
    smem = pl.BlockSpec(memory_space=pltpu.SMEM)
    vmem = pl.BlockSpec(memory_space=pltpu.VMEM)
    hbm = pl.BlockSpec(memory_space=pl.ANY)
    return pl.pallas_call(
        functools.partial(product_kernel, g),
        out_shape=jax.ShapeDtypeStruct((NCR * g.rows, BS, NCR * BS), F32),
        in_specs=[smem] * 4 + [vmem] * 2 + [hbm] * 2,
        out_specs=vmem,
        scratch_shapes=[
            pltpu.VMEM(gy.shape, F32),
            pltpu.VMEM(gz.shape, F32),
            pltpu.SMEM((g.cols, 8, 128), F32),
            pltpu.VMEM((n_i * n_k, 3 * BS, NCR * BS), BF16),
            pltpu.SemaphoreType.DMA((3,)),
        ],
        compiler_params=pltpu.CompilerParams(vmem_limit_bytes=32 << 20),
        name="product",
    )(requests, slots, counts, rows, blocks, restrict, gy, gz)


def reduce_kernel(g, acc_ref, o_ref, r1, s1, r2, s1_send, s1_recv, s2_send, s2_recv):
    me_r, me_c = lax.axis_index("row"), lax.axis_index("col")
    x, z = me_c // g.z, me_c % g.z
    per = acc_ref.shape[0] // g.cols
    barrier = pltpu.get_barrier_semaphore()

    def col_x(dx):
        return ((x + dx) % g.x) * g.z + z

    def col_z(dz):
        return x * g.z + (z + dz) % g.z

    for dx in range(1, g.x):
        pl.semaphore_signal(barrier, inc=1, device_id=(me_r, col_x(dx)), device_id_type=MESH)
    for dz in range(1, g.z):
        pl.semaphore_signal(barrier, inc=1, device_id=(me_r, col_z(dz)), device_id_type=MESH)
    pl.semaphore_wait(barrier, g.x + g.z - 2)

    order = sorted(range(g.z), key=lambda dz: -min(dz, g.z - dz))
    first = []
    for dz in order:
        for dx in range(1, g.x):
            tile = ((x + dx) % g.x) * g.z + (z + dz) % g.z
            copy = pltpu.make_async_remote_copy(
                src_ref=acc_ref.at[pl.ds(tile * per, per)], dst_ref=r1.at[dz, dx - 1],
                send_sem=s1_send.at[dz, dx - 1], recv_sem=s1_recv.at[dz, dx - 1],
                device_id=(me_r, col_x(dx)), device_id_type=MESH,
            )
            copy.start()
            first.append((dz, copy))
    second = []
    for dz in order:
        for at, copy in first:
            if at == dz:
                copy.wait_recv()
        tile = x * g.z + (z + dz) % g.z
        total = acc_ref[pl.ds(tile * per, per)]
        for dx in range(1, g.x):
            total = total + r1[dz, dx - 1]
        s1[dz] = total
        if dz:
            copy = pltpu.make_async_remote_copy(
                src_ref=s1.at[dz], dst_ref=r2.at[dz - 1],
                send_sem=s2_send.at[dz - 1], recv_sem=s2_recv.at[dz - 1],
                device_id=(me_r, col_z(dz)), device_id_type=MESH,
            )
            copy.start()
            second.append((dz, copy))
    total = s1[0]
    for dz, copy in second:
        copy.wait_recv()
        total = total + r2[dz - 1]
    o_ref[...] = total
    for _, copy in first + second:
        copy.wait_send()


def reduce(g, acc):
    tile = acc.shape[1:]
    per = acc.shape[0] // g.cols
    vmem = pl.BlockSpec(memory_space=pltpu.VMEM)
    dma = pltpu.SemaphoreType.DMA
    return pl.pallas_call(
        functools.partial(reduce_kernel, g),
        out_shape=jax.ShapeDtypeStruct((per,) + tile, F32),
        in_specs=[vmem],
        out_specs=vmem,
        scratch_shapes=[
            pltpu.VMEM((g.z, max(g.x - 1, 1), per) + tile, F32),
            pltpu.VMEM((g.z, per) + tile, F32),
            pltpu.VMEM((g.z - 1, per) + tile, F32),
            dma((g.z, max(g.x - 1, 1))), dma((g.z, max(g.x - 1, 1))),
            dma((g.z - 1,)), dma((g.z - 1,)),
        ],
        compiler_params=pltpu.CompilerParams(collective_id=1, has_side_effects=True),
        name="reduce",
    )(acc)


def request_tables(g, requests):
    owner_row = requests // (FBD * g.cols)
    inside = requests % FBD
    turn = (owner_row - lax.axis_index("row") + g.rows) % g.rows
    idxy = jnp.concatenate([owner_row * FBD + inside, turn * FBD + inside], axis=1)
    idxy = jnp.pad(idxy, ((0, 0), (0, 128 - 2 * g.slot)))[:, None, :]
    zz = (jnp.arange(g.cols, dtype=jnp.int32) % g.z)[:, None]
    at = zz * FBD + inside
    per = g.z // g.pair * g.slot
    owner_row = owner_row.reshape(1, g.x, g.pair, per)
    at = at.reshape(1, g.x, g.pair, per)
    rows = jnp.arange(g.rows, dtype=jnp.int32)[:, None, None, None]
    idxz = jnp.where(owner_row == rows, at, 0).sum(axis=-1)
    idxz = jnp.pad(idxz.reshape(g.rows * g.x, g.pair), ((0, 0), (0, 128 - g.pair)))[:, None, :]
    return idxy, idxz


def local(
    g,
    operator_blocks,
    operator_count,
    operator_slot,
    fetch_lists,
    prolong_blocks,
    prolong_cols,
    restrict_blocks,
    restrict_rows,
):
    requests = fetch_lists.reshape(g.cols, g.slot)
    idxy, idxz = request_tables(g, requests)
    tags = jnp.repeat(prolong_cols.astype(F32), BS, axis=1)[:, None, :]
    gy, gz = fetch(g, idxy, idxz, prolong_blocks, tags)
    acc = product(
        g, requests, operator_slot, operator_count, restrict_rows, operator_blocks, restrict_blocks, gy, gz
    )
    share = reduce(g, acc)
    return share.reshape(-1, NCR * BS).T


def solution(mesh):
    g = Geometry(mesh.shape["row"], mesh.shape["col"])
    return jax.shard_map(
        functools.partial(local, g),
        mesh=mesh,
        in_specs=(
            P(("row", "col"), None, None),
            P(("row", "col")),
            P(("row", "col"), None),
            P("row", "col", None, None),
            P(("row", "col"), None, None),
            P(("row", "col"), None),
            P(("row", "col"), None, None),
            P(("row", "col"), None),
        ),
        out_specs=P("row", "col"),
        check_vma=False,
    )
```

```python
import functools

import jax
import jax.numpy as jnp
from jax import lax
from jax.experimental import pallas as pl
from jax.experimental.pallas import tpu as pltpu
from jax.sharding import PartitionSpec as P

MESH = pl.DeviceIdType.MESH
F32 = jnp.float32
BF16 = jnp.bfloat16

NX, NZ = 4, 8
CORES = 2
NCR = 2
FBD = 8
SLOT = 4
BS = 64
VMEM = 63 << 20
CHUNKS = 2
PART = BS // (2 * CHUNKS)


class Geometry:
    def __init__(self, rows, cols, x=NX, z=NZ, slot=SLOT):
        self.rows, self.cols, self.x, self.z, self.slot = rows, cols, x, z, slot
        self.y = rows // CORES
        self.span = rows // slot
        self.pair = z // self.span
        self.n_y, self.n_z = cols, rows * x
        self.out_y = [slot * PART + (8 if ch == 0 else 0) for ch in range(CHUNKS)]
        self.out_z = [self.pair * PART for _ in range(CHUNKS)]


def half_ring(n):
    return n // 2, n - 1 - n // 2


def split(value):
    high = value.astype(BF16)
    return high, (value - high.astype(F32)).astype(BF16)


def dot_t(left, right):
    return lax.dot_general(left, right, (((0,), (0,)), ((), ())), preferred_element_type=F32)


class Ring:
    def __init__(self, steps, sign, send, recv, make):
        self.steps, self.sign, self.send, self.recv, self.make = steps, sign, send, recv, make

    def copy(self, t):
        return self.make(t, self.sign, self.send.at[t - 1], self.recv.at[t - 1])


def fetch_kernel(g, fl_ref, cols_hbm, p_hbm, *refs):
    gy_refs, gz_refs, st_y, st_z, pan_y, pan_z = (refs[n * CHUNKS:(n + 1) * CHUNKS] for n in range(6))
    (
        pay_y, pay_z, tab, smem_y, smem_z, cols,
        up_s, up_r, down_s, down_r, zup_s, zup_r, zdown_s, zdown_r, sib_s, sib_r, tab_s, tab_r, ex_s, ex_r, loc,
    ) = refs[6 * CHUNKS:]
    me_r, me_c = lax.axis_index("row"), lax.axis_index("col")
    y, core = me_r // CORES, me_r % CORES
    x, z = me_c // g.z, me_c % g.z

    def remote(src, dst, send, recv, device):
        return pltpu.make_async_remote_copy(
            src_ref=src, dst_ref=dst, send_sem=send, recv_sem=recv, device_id=device, device_id_type=MESH
        )

    def row_of(yy):
        return ((yy + g.y) % g.y) * CORES + core

    def col_of(xx, zz):
        return ((xx + g.x) % g.x) * g.z + (zz + g.z) % g.z

    own = []
    for ch in range(CHUNKS):
        top, bottom = ch * PART, (CHUNKS + ch) * PART
        own.append(pltpu.make_async_copy(
            p_hbm.at[:, pl.ds(top, PART), :], pan_y[ch].at[pl.ds(me_r * FBD, FBD)], loc.at[2 * ch]))
        own.append(pltpu.make_async_copy(
            p_hbm.at[:, pl.ds(bottom, PART), :], pan_z[ch].at[pl.ds(z * FBD, FBD)], loc.at[2 * ch + 1]))
    base = 2 * CHUNKS
    tag_in = pltpu.make_async_copy(cols_hbm, cols, loc.at[base])

    barrier = pltpu.get_barrier_semaphore()
    near = [(row_of(y + 1), me_c), (row_of(y - 1), me_c), (y * CORES + (1 - core), me_c)]
    near += [(me_r, col_of(x, z + 1)), (me_r, col_of(x, z - 1))]
    near += [(me_r, col_of(x + dx, z)) for dx in range(1, g.x)]
    for device in near:
        pl.semaphore_signal(barrier, inc=1, device_id=device, device_id_type=MESH)
    for copy in own + [tag_in]:
        copy.start()
    table = jnp.concatenate([fl_ref[s:s + 1, :] for s in range(g.slot)], axis=1)
    if table.shape[1] < 128:
        table = jnp.pad(table, ((0, 0), (0, 128 - table.shape[1])))
    tab[0] = table
    tag_in.wait()
    lane = lax.broadcasted_iota(jnp.int32, (1, 128), 1) // BS
    pay_y[me_r, 0:8, :] = jnp.zeros((8, 128), jnp.int32)
    pay_z[z] = jnp.zeros((8, 128), jnp.int32)
    for j in range(FBD):
        pay_y[me_r, 8 + j:9 + j, :] = jnp.where(lane == 0, cols[0, j], cols[1, j])
    for copy in own:
        copy.wait()
    pl.semaphore_wait(barrier, len(near))

    def rings_of(buf_y, buf_z, unit):
        def make_y(t, sign, send, recv):
            view = buf_y.at[pl.ds(row_of(y - sign * (t - 1)) * unit, unit)]
            return remote(view, view, send, recv, (row_of(y + sign), me_c))

        def make_z(t, sign, send, recv):
            view = buf_z.at[pl.ds((z - sign * (t - 1) + g.z) % g.z * unit, unit)]
            return remote(view, view, send, recv, (me_r, col_of(x, z + sign)))

        return make_y, make_z

    class Gather:
        def __init__(self, which, buf_y, buf_z, unit):
            make_y, make_z = rings_of(buf_y, buf_z, unit)
            (up_y, down_y), (up_z, down_z) = (half_ring(n)[::-1 if which % 2 else 1] for n in (g.y, g.z))
            self.y_rings = [
                Ring(up_y, 1, up_s.at[which], up_r.at[which], make_y),
                Ring(down_y, -1, down_s.at[which], down_r.at[which], make_y),
            ]
            self.z_rings = [
                Ring(up_z, 1, zup_s.at[which], zup_r.at[which], make_z),
                Ring(down_z, -1, zdown_s.at[which], zdown_r.at[which], make_z),
            ]
            self.rings = [self.y_rings[0], self.z_rings[0], self.y_rings[1], self.z_rings[1]]
            self.which, self.buf, self.unit, self.sibs = which, buf_y, unit, []

        def sibling(self, yy):
            n = len(self.sibs)
            view = self.buf.at[pl.ds(row_of(yy) * self.unit, self.unit)]
            copy = remote(
                view, view, sib_s.at[self.which, n], sib_r.at[self.which, n], (y * CORES + (1 - core), me_c))
            copy.start()
            self.sibs.append(copy)

        def begin(self):
            for ring in self.rings:
                if ring.steps:
                    ring.copy(1).start()
            self.sibling(y)

        def advance(self, t):
            for ring in self.rings:
                if t <= ring.steps:
                    ring.copy(t).wait_recv()
                    if t < ring.steps:
                        ring.copy(t + 1).start()
                    if ring in self.y_rings:
                        self.sibling(y - ring.sign * t)

        def finish(self):
            for copy in self.sibs:
                copy.wait_recv()

        def drain(self):
            for ring in self.rings:
                for t in range(1, ring.steps + 1):
                    ring.copy(t).wait_send()
            for copy in self.sibs:
                copy.wait_send()

    gathers = [Gather(ch, pan_y[ch], pan_z[ch], FBD) for ch in range(CHUNKS)]
    lists = Gather(CHUNKS, pay_y, pay_z, 1)
    steps = max(g.y, g.z) // 2

    for dx in range(1, g.x):
        remote(tab.at[0], tab.at[dx], tab_s.at[dx - 1], tab_r.at[dx - 1], (me_r, col_of(x + dx, z))).start()
    gathers[0].begin()
    for dx in range(g.x):
        if dx:
            remote(tab.at[0], tab.at[dx], tab_s.at[dx - 1], tab_r.at[dx - 1], (me_r, col_of(x + dx, z))).wait_recv()
        pay_y[me_r, dx:dx + 1, :] = tab[dx]
        pay_z[z, dx:dx + 1, :] = tab[dx]
    lists.begin()
    for ch in range(1, CHUNKS):
        gathers[ch].begin()
    to_smem = [
        pltpu.make_async_copy(pay_z, smem_y, loc.at[base + 1]),
        pltpu.make_async_copy(pay_y.at[:, 0:8, :], smem_z, loc.at[base + 2]),
    ]
    for t in range(1, steps + 1):
        lists.advance(t)
        if t == steps:
            lists.finish()
            for copy in to_smem:
                copy.start()
        gathers[0].advance(t)
        for ch in range(1, CHUNKS):
            if t < steps:
                gathers[ch].advance(t)
    gathers[0].finish()
    for copy in to_smem:
        copy.wait()

    eight = lax.broadcasted_iota(jnp.int32, (8, 128), 0)

    def send_y(ch, t, away):
        dx, dz = t // g.z, t % g.z
        from_z, from_x = (z + dz) % g.z, (g.x - dx) % g.x
        for s in range(g.slot):
            block = smem_y[from_z, from_x, s * g.cols + me_c]
            owner_row, inside = block // (FBD * g.cols), block % FBD
            st_y[ch][t, s * PART:(s + 1) * PART, :] = pan_y[ch][owner_row * FBD + inside]
            if ch == 0:
                tags = jnp.where(eight == inside, pay_y[owner_row, 8:16, :], 0).astype(F32)
                tag = jnp.sum(tags, axis=0, keepdims=True)
                for rep in range(8 // g.slot):
                    row = g.slot * PART + rep * g.slot + s
                    st_y[ch][t, row:row + 1, :] = tag
        if away:
            device = (me_r, col_of(x + dx, z + dz))
            remote(st_y[ch].at[t], gy_refs[ch].at[t], ex_s.at[0, ch], ex_r.at[0, ch], device).start()

    def send_z(ch, t, away):
        dr, dx = t // g.x, t % g.x
        to_row, from_x = (me_r + dr) % g.rows, (g.x - dx) % g.x
        first = smem_z[to_row, from_x, 0] // (FBD * g.cols)
        turn = (me_r - first + g.rows) % g.rows
        s, zz = turn % g.slot, turn // g.slot
        for j in range(g.pair):
            at = zz + g.span * j
            block = smem_z[to_row, from_x, s * g.cols + x * g.z + at]
            st_z[ch][t, j * PART:(j + 1) * PART, :] = pan_z[ch][at * FBD + block % FBD]
        if away:
            device = (to_row, col_of(x + dx, z))
            remote(st_z[ch].at[t], gz_refs[ch].at[t], ex_s.at[1, ch], ex_r.at[1, ch], device).start()

    ratio = g.n_z // g.n_y
    last = []
    for ch in range(CHUNKS):
        for j in range(1, ratio):
            send_z(ch, (j * 29) % g.n_z, True)

        @pl.loop(1, g.n_y)
        def _(q):
            send_y(ch, (q * 13) % g.n_y, True)
            for j in range(ratio):
                send_z(ch, ((ratio * q + j) * 29) % g.n_z, True)

        send_y(ch, 0, False)
        send_z(ch, 0, False)
        for which, (src, dst) in enumerate(((st_y, gy_refs), (st_z, gz_refs))):
            copy = pltpu.make_async_copy(src[ch].at[0], dst[ch].at[0], loc.at[base + 3 + 2 * ch + which])
            copy.start()
            last.append(copy)
        if ch + 1 < CHUNKS:
            gathers[ch + 1].advance(steps)
            gathers[ch + 1].finish()

    for copy in last:
        copy.wait()
    for dx in range(1, g.x):
        remote(tab.at[0], tab.at[dx], tab_s.at[dx - 1], tab_r.at[dx - 1], (me_r, col_of(x + dx, z))).wait_send()
    lists.drain()
    for gather in gathers:
        gather.drain()
    for ch in range(CHUNKS):
        for which, (src, dst, n) in enumerate(((st_y, gy_refs, g.n_y), (st_z, gz_refs, g.n_z))):
            view_s, view_d = src[ch].at[pl.ds(1, n - 1)], dst[ch].at[pl.ds(1, n - 1)]
            rest = remote(view_s, view_d, ex_s.at[which, ch], ex_r.at[which, ch], (me_r, col_of(x, z + 1)))
            rest.wait_send()
            rest.wait_recv()


def fetch(g, requests, cols, prolong_blocks):
    far_y, far_z = max(half_ring(g.y)), max(half_ring(g.z))
    dma = pltpu.SemaphoreType.DMA
    hbm = pl.BlockSpec(memory_space=pltpu.HBM)
    got = [jax.ShapeDtypeStruct((g.n_y, n, 128), F32) for n in g.out_y]
    got += [jax.ShapeDtypeStruct((g.n_z, n, 128), F32) for n in g.out_z]
    kinds = CHUNKS + 1
    return pl.pallas_call(
        functools.partial(fetch_kernel, g),
        out_shape=tuple(got),
        in_specs=[pl.BlockSpec(memory_space=pltpu.VMEM), hbm, hbm],
        out_specs=(hbm,) * (2 * CHUNKS),
        scratch_shapes=[
            *[pltpu.VMEM(s.shape, F32) for s in got],
            *[pltpu.VMEM((g.rows * FBD, PART, 128), F32) for _ in range(CHUNKS)],
            *[pltpu.VMEM((g.z * FBD, PART, 128), F32) for _ in range(CHUNKS)],
            pltpu.VMEM((g.rows, 16, 128), jnp.int32),
            pltpu.VMEM((g.z, 8, 128), jnp.int32),
            pltpu.VMEM((g.x, 1, 128), jnp.int32),
            pltpu.SMEM((g.z, 8, 128), jnp.int32),
            pltpu.SMEM((g.rows, 8, 128), jnp.int32),
            pltpu.SMEM(cols.shape, jnp.int32),
            dma((kinds, far_y)), dma((kinds, far_y)), dma((kinds, far_y)), dma((kinds, far_y)),
            dma((kinds, far_z)), dma((kinds, far_z)), dma((kinds, far_z)), dma((kinds, far_z)),
            dma((kinds, g.y)), dma((kinds, g.y)),
            dma((max(g.x - 1, 1),)), dma((max(g.x - 1, 1),)),
            dma((2, CHUNKS)), dma((2, CHUNKS)), dma((4 * CHUNKS + 3,)),
        ],
        compiler_params=pltpu.CompilerParams(
            collective_id=0, has_side_effects=True, vmem_limit_bytes=VMEM
        ),
        name="fetch",
    )(requests, cols, prolong_blocks)


def product_kernel(g, n_i, n_k, fetch_hbm, slot_hbm, count_hbm, rows_hbm, a_hbm, r_hbm, *refs):
    got_hbm, refs = refs[:2 * CHUNKS], refs[2 * CHUNKS:]
    acc_ref, got, refs = refs[0], refs[1:1 + 2 * CHUNKS], refs[1 + 2 * CHUNKS:]
    w, a_ref, r_ref, requests, slots, count, rows, tags, sem, a_sem = refs
    me_r, me_c = lax.axis_index("row"), lax.axis_index("col")
    x, z = me_c // g.z, me_c % g.z
    early = [
        pltpu.make_async_copy(rows_hbm, rows, sem.at[0]),
        pltpu.make_async_copy(count_hbm, count, sem.at[1]),
        pltpu.make_async_copy(r_hbm, r_ref, sem.at[2]),
    ]
    late = [
        pltpu.make_async_copy(slot_hbm, slots, sem.at[3]),
        pltpu.make_async_copy(fetch_hbm, requests, sem.at[4]),
        pltpu.make_async_copy(got_hbm[0].at[:, pl.ds(g.slot * PART, 8), :], tags, sem.at[5]),
    ]
    late += [pltpu.make_async_copy(src, dst, sem.at[6 + n]) for n, (src, dst) in enumerate(zip(got_hbm, got))]

    def block_row(i):
        return pltpu.make_async_copy(a_hbm.at[i], a_ref.at[i], a_sem.at[i])

    for copy in early:
        copy.start()
    for i in range(n_i):
        block_row(i).start()
    for copy in late:
        copy.start()
    acc_ref[...] = jnp.zeros_like(acc_ref)
    half = lax.broadcasted_iota(jnp.int32, (BS, 2 * BS), 1) // BS
    for copy in early:
        copy.wait()

    @pl.loop(0, n_i)
    def _(i):
        block_row(i).wait()
        stored = r_ref[i]
        swapped = pltpu.roll(stored, BS, 1)
        first, second = rows[0, i], rows[1, i]
        mine = jnp.where(half == 0, first, second)
        other = jnp.where(half == 0, second, first)
        dense = jnp.where(mine == half, stored, 0.0) + jnp.where(other == half, swapped, 0.0)
        r_hi, r_lo = split(dense)
        a_hi, a_lo = split(a_ref[i])
        ra = dot_t(
            jnp.concatenate([a_hi, a_lo, a_hi], axis=0),
            jnp.concatenate([r_hi, r_hi, r_lo], axis=0),
        )
        for k in range(n_k):
            part = jnp.where(k < count[i], ra[k * BS:(k + 1) * BS, :], 0.0)
            hi, lo = split(part)
            w[i * n_k + k, 0:BS, :] = hi
            w[i * n_k + k, BS:2 * BS, :] = lo

    for copy in late:
        copy.wait()

    @pl.loop(0, n_i)
    def _(i):
        for k in range(n_k):
            slot = slots[i, k]
            peer, s = slot // g.slot, slot % g.slot
            px, pz = peer // g.z, peer % g.z
            owner_row = requests[s, peer] // (FBD * g.cols)
            dx = (x - px + g.x) % g.x
            t = dx * g.z + (z - pz + g.z) % g.z
            tz = ((me_r - owner_row + g.rows) % g.rows) * g.x + dx
            j = pz // g.span
            top = [got[ch][t, pl.ds(pl.multiple_of(s * PART, 8), PART), :] for ch in range(CHUNKS)]
            bottom = [got[CHUNKS + ch][tz, pl.ds(pl.multiple_of(j * PART, 8), PART), :] for ch in range(CHUNKS)]
            p_hi, p_lo = split(jnp.concatenate(top + bottom, axis=0))
            w_hi, w_lo = w[i * n_k + k, 0:BS, :], w[i * n_k + k, BS:2 * BS, :]
            out = dot_t(jnp.concatenate([p_hi, p_lo, p_hi], axis=0), jnp.concatenate([w_hi, w_hi, w_lo], axis=0))
            first = tags[t, s, 0].astype(jnp.int32)
            second = tags[t, s, BS].astype(jnp.int32)
            acc_ref[first] += out[0:BS, :]
            acc_ref[second] += out[BS:2 * BS, :]


def product(g, requests, slots, counts, rows, blocks, restrict, got):
    n_i, n_k = slots.shape
    hbm = pl.BlockSpec(memory_space=pltpu.HBM)
    return pl.pallas_call(
        functools.partial(product_kernel, g, n_i, n_k),
        out_shape=jax.ShapeDtypeStruct((NCR * g.rows, BS, NCR * BS), F32),
        in_specs=[hbm] * (6 + 2 * CHUNKS),
        out_specs=pl.BlockSpec(memory_space=pltpu.VMEM),
        scratch_shapes=[
            *[pltpu.VMEM(a.shape, F32) for a in got],
            pltpu.VMEM((n_i * n_k, 2 * BS, NCR * BS), BF16),
            pltpu.VMEM(blocks.shape, F32),
            pltpu.VMEM(restrict.shape, F32),
            pltpu.SMEM(requests.shape, jnp.int32),
            pltpu.SMEM(slots.shape, jnp.int32),
            pltpu.SMEM(counts.shape, jnp.int32),
            pltpu.SMEM(rows.shape, jnp.int32),
            pltpu.SMEM((g.cols, 8, 128), F32),
            pltpu.SemaphoreType.DMA((6 + 2 * CHUNKS,)),
            pltpu.SemaphoreType.DMA((n_i,)),
        ],
        compiler_params=pltpu.CompilerParams(vmem_limit_bytes=VMEM),
        name="product",
    )(requests, slots, counts, rows, blocks, restrict, *got)


def reduce_kernel(g, acc_ref, o_ref, r1, s1, r2, s1_send, s1_recv, s2_send, s2_recv):
    me_r, me_c = lax.axis_index("row"), lax.axis_index("col")
    x, z = me_c // g.z, me_c % g.z
    per = acc_ref.shape[0] // g.cols
    barrier = pltpu.get_barrier_semaphore()

    def col_x(dx):
        return ((x + dx) % g.x) * g.z + z

    def col_z(dz):
        return x * g.z + (z + dz) % g.z

    for dx in range(1, g.x):
        pl.semaphore_signal(barrier, inc=1, device_id=(me_r, col_x(dx)), device_id_type=MESH)
    for dz in range(1, g.z):
        pl.semaphore_signal(barrier, inc=1, device_id=(me_r, col_z(dz)), device_id_type=MESH)
    pl.semaphore_wait(barrier, g.x + g.z - 2)

    order = sorted(range(g.z), key=lambda dz: -min(dz, g.z - dz))
    first = []
    for dz in order:
        for dx in range(1, g.x):
            tile = ((x + dx) % g.x) * g.z + (z + dz) % g.z
            copy = pltpu.make_async_remote_copy(
                src_ref=acc_ref.at[pl.ds(tile * per, per)], dst_ref=r1.at[dz, dx - 1],
                send_sem=s1_send.at[dz, dx - 1], recv_sem=s1_recv.at[dz, dx - 1],
                device_id=(me_r, col_x(dx)), device_id_type=MESH,
            )
            copy.start()
            first.append((dz, copy))
    second = []
    for dz in order:
        for at, copy in first:
            if at == dz:
                copy.wait_recv()
        tile = x * g.z + (z + dz) % g.z
        total = acc_ref[pl.ds(tile * per, per)]
        for dx in range(1, g.x):
            total = total + r1[dz, dx - 1]
        s1[dz] = total
        if dz:
            copy = pltpu.make_async_remote_copy(
                src_ref=s1.at[dz], dst_ref=r2.at[dz - 1],
                send_sem=s2_send.at[dz - 1], recv_sem=s2_recv.at[dz - 1],
                device_id=(me_r, col_z(dz)), device_id_type=MESH,
            )
            copy.start()
            second.append((dz, copy))
    total = s1[0]
    for dz, copy in second:
        copy.wait_recv()
        total = total + r2[dz - 1]
    o_ref[...] = total
    for _, copy in first + second:
        copy.wait_send()


def reduce(g, acc):
    tile = acc.shape[1:]
    per = acc.shape[0] // g.cols
    vmem = pl.BlockSpec(memory_space=pltpu.VMEM)
    dma = pltpu.SemaphoreType.DMA
    return pl.pallas_call(
        functools.partial(reduce_kernel, g),
        out_shape=jax.ShapeDtypeStruct((per,) + tile, F32),
        in_specs=[vmem],
        out_specs=vmem,
        scratch_shapes=[
            pltpu.VMEM((g.z, max(g.x - 1, 1), per) + tile, F32),
            pltpu.VMEM((g.z, per) + tile, F32),
            pltpu.VMEM((g.z - 1, per) + tile, F32),
            dma((g.z, max(g.x - 1, 1))), dma((g.z, max(g.x - 1, 1))),
            dma((g.z - 1,)), dma((g.z - 1,)),
        ],
        compiler_params=pltpu.CompilerParams(collective_id=1, has_side_effects=True),
        name="reduce",
    )(acc)


def local(
    g,
    operator_blocks,
    operator_count,
    operator_slot,
    fetch_lists,
    prolong_blocks,
    prolong_cols,
    restrict_blocks,
    restrict_rows,
):
    requests = fetch_lists.reshape(g.cols, g.slot).T
    got = fetch(g, requests, prolong_cols.T, prolong_blocks)
    acc = product(
        g, requests, operator_slot, operator_count, restrict_rows.T, operator_blocks, restrict_blocks, got
    )
    share = reduce(g, acc)
    return share.reshape(-1, NCR * BS).T


def solution(mesh):
    g = Geometry(mesh.shape["row"], mesh.shape["col"])
    return jax.shard_map(
        functools.partial(local, g),
        mesh=mesh,
        in_specs=(
            P(("row", "col"), None, None),
            P(("row", "col")),
            P(("row", "col"), None),
            P("row", "col", None, None),
            P(("row", "col"), None, None),
            P(("row", "col"), None),
            P(("row", "col"), None, None),
            P(("row", "col"), None),
        ),
        out_specs=P("row", "col"),
        check_vma=False,
    )
```

```python
import functools

import jax
import jax.numpy as jnp
from jax import lax
from jax.experimental import pallas as pl
from jax.experimental.pallas import tpu as pltpu
from jax.sharding import PartitionSpec as P

MESH = pl.DeviceIdType.MESH
F32 = jnp.float32
BF16 = jnp.bfloat16

NX, NZ = 4, 8
CORES = 2
NCR = 2
FBD = 8
SLOT = 4
BS = 64
VMEM = 63 << 20
CHUNKS = 2
PART = BS // (2 * CHUNKS)


class Geometry:
    def __init__(self, rows, cols, x=NX, z=NZ, slot=SLOT):
        self.rows, self.cols, self.x, self.z, self.slot = rows, cols, x, z, slot
        self.y = rows // CORES
        self.span = rows // slot
        self.pair = z // self.span
        self.n_y, self.n_z = cols, rows * x
        self.out_y = [slot * PART + (8 if ch == 0 else 0) for ch in range(CHUNKS)]
        self.out_z = [self.pair * PART for _ in range(CHUNKS)]


def half_ring(n):
    return n // 2, n - 1 - n // 2


def split(value):
    high = value.astype(BF16)
    return high, (value - high.astype(F32)).astype(BF16)


def dot_t(left, right):
    return lax.dot_general(left, right, (((0,), (0,)), ((), ())), preferred_element_type=F32)


class Ring:
    def __init__(self, steps, sign, send, recv, make):
        self.steps, self.sign, self.send, self.recv, self.make = steps, sign, send, recv, make

    def copy(self, t):
        return self.make(t, self.sign, self.send.at[t - 1], self.recv.at[t - 1])


def fetch_kernel(g, fl_ref, cols_hbm, p_hbm, *refs):
    gy_refs, gz_refs, st_y, st_z, pan_y, pan_z = (refs[n * CHUNKS:(n + 1) * CHUNKS] for n in range(6))
    (
        pay_y, pay_z, tab, smem_y, smem_z, cols,
        up_s, up_r, down_s, down_r, zup_s, zup_r, zdown_s, zdown_r, sib_s, sib_r, tab_s, tab_r, ex_s, ex_r, loc,
    ) = refs[6 * CHUNKS:]
    me_r, me_c = lax.axis_index("row"), lax.axis_index("col")
    y, core = me_r // CORES, me_r % CORES
    x, z = me_c // g.z, me_c % g.z

    def remote(src, dst, send, recv, device):
        return pltpu.make_async_remote_copy(
            src_ref=src, dst_ref=dst, send_sem=send, recv_sem=recv, device_id=device, device_id_type=MESH
        )

    def row_of(yy):
        return ((yy + g.y) % g.y) * CORES + core

    def col_of(xx, zz):
        return ((xx + g.x) % g.x) * g.z + (zz + g.z) % g.z

    own = []
    for ch in range(CHUNKS):
        top, bottom = ch * PART, (CHUNKS + ch) * PART
        own.append(pltpu.make_async_copy(
            p_hbm.at[:, pl.ds(top, PART), :], pan_y[ch].at[pl.ds(me_r * FBD, FBD)], loc.at[2 * ch]))
        own.append(pltpu.make_async_copy(
            p_hbm.at[:, pl.ds(bottom, PART), :], pan_z[ch].at[pl.ds(z * FBD, FBD)], loc.at[2 * ch + 1]))
    base = 2 * CHUNKS
    tag_in = pltpu.make_async_copy(cols_hbm, cols, loc.at[base])

    barrier = pltpu.get_barrier_semaphore()
    near = [(row_of(y + 1), me_c), (row_of(y - 1), me_c), (y * CORES + (1 - core), me_c)]
    near += [(me_r, col_of(x, z + 1)), (me_r, col_of(x, z - 1))]
    near += [(me_r, col_of(x + dx, z)) for dx in range(1, g.x)]
    for device in near:
        pl.semaphore_signal(barrier, inc=1, device_id=device, device_id_type=MESH)
    for copy in own + [tag_in]:
        copy.start()
    table = jnp.concatenate([fl_ref[s:s + 1, :] for s in range(g.slot)], axis=1)
    if table.shape[1] < 128:
        table = jnp.pad(table, ((0, 0), (0, 128 - table.shape[1])))
    tab[0] = table
    tag_in.wait()
    lane = lax.broadcasted_iota(jnp.int32, (1, 128), 1) // BS
    pay_y[me_r, 0:8, :] = jnp.zeros((8, 128), jnp.int32)
    pay_z[z] = jnp.zeros((8, 128), jnp.int32)
    for j in range(FBD):
        pay_y[me_r, 8 + j:9 + j, :] = jnp.where(lane == 0, cols[0, j], cols[1, j])
    for copy in own:
        copy.wait()
    pl.semaphore_wait(barrier, len(near))

    def rings_of(buf_y, buf_z, unit):
        def make_y(t, sign, send, recv):
            view = buf_y.at[pl.ds(row_of(y - sign * (t - 1)) * unit, unit)]
            return remote(view, view, send, recv, (row_of(y + sign), me_c))

        def make_z(t, sign, send, recv):
            view = buf_z.at[pl.ds((z - sign * (t - 1) + g.z) % g.z * unit, unit)]
            return remote(view, view, send, recv, (me_r, col_of(x, z + sign)))

        return make_y, make_z

    class Gather:
        def __init__(self, which, buf_y, buf_z, unit):
            make_y, make_z = rings_of(buf_y, buf_z, unit)
            (up_y, down_y), (up_z, down_z) = (half_ring(n)[::-1 if which % 2 else 1] for n in (g.y, g.z))
            self.y_rings = [
                Ring(up_y, 1, up_s.at[which], up_r.at[which], make_y),
                Ring(down_y, -1, down_s.at[which], down_r.at[which], make_y),
            ]
            self.z_rings = [
                Ring(up_z, 1, zup_s.at[which], zup_r.at[which], make_z),
                Ring(down_z, -1, zdown_s.at[which], zdown_r.at[which], make_z),
            ]
            self.rings = [self.y_rings[0], self.z_rings[0], self.y_rings[1], self.z_rings[1]]
            self.which, self.buf, self.unit, self.sibs = which, buf_y, unit, []

        def sibling(self, yy):
            n = len(self.sibs)
            view = self.buf.at[pl.ds(row_of(yy) * self.unit, self.unit)]
            copy = remote(
                view, view, sib_s.at[self.which, n], sib_r.at[self.which, n], (y * CORES + (1 - core), me_c))
            copy.start()
            self.sibs.append(copy)

        def begin(self):
            for ring in self.rings:
                if ring.steps:
                    ring.copy(1).start()
            self.sibling(y)

        def advance(self, t):
            for ring in self.rings:
                if t <= ring.steps:
                    ring.copy(t).wait_recv()
                    if t < ring.steps:
                        ring.copy(t + 1).start()
                    if ring in self.y_rings:
                        self.sibling(y - ring.sign * t)

        def finish(self):
            for copy in self.sibs:
                copy.wait_recv()

        def drain(self):
            for ring in self.rings:
                for t in range(1, ring.steps + 1):
                    ring.copy(t).wait_send()
            for copy in self.sibs:
                copy.wait_send()

    gathers = [Gather(ch, pan_y[ch], pan_z[ch], FBD) for ch in range(CHUNKS)]
    lists = Gather(CHUNKS, pay_y, pay_z, 1)
    steps = max(g.y, g.z) // 2

    for dx in range(1, g.x):
        remote(tab.at[0], tab.at[dx], tab_s.at[dx - 1], tab_r.at[dx - 1], (me_r, col_of(x + dx, z))).start()
    gathers[0].begin()
    for dx in range(g.x):
        if dx:
            remote(tab.at[0], tab.at[dx], tab_s.at[dx - 1], tab_r.at[dx - 1], (me_r, col_of(x + dx, z))).wait_recv()
        pay_y[me_r, dx:dx + 1, :] = tab[dx]
        pay_z[z, dx:dx + 1, :] = tab[dx]
    lists.begin()
    for ch in range(1, CHUNKS):
        gathers[ch].begin()
    to_smem = [
        pltpu.make_async_copy(pay_z, smem_y, loc.at[base + 1]),
        pltpu.make_async_copy(pay_y.at[:, 0:8, :], smem_z, loc.at[base + 2]),
    ]
    for t in range(1, steps + 1):
        lists.advance(t)
        if t == steps:
            lists.finish()
            for copy in to_smem:
                copy.start()
        gathers[0].advance(t)
        for ch in range(1, CHUNKS):
            if t < steps:
                gathers[ch].advance(t)
    gathers[0].finish()
    for copy in to_smem:
        copy.wait()

    eight = lax.broadcasted_iota(jnp.int32, (8, 128), 0)

    def send_y(ch, t, away):
        dx, dz = t // g.z, t % g.z
        from_z, from_x = (z + dz) % g.z, (g.x - dx) % g.x
        for s in range(g.slot):
            block = smem_y[from_z, from_x, s * g.cols + me_c]
            owner_row, inside = block // (FBD * g.cols), block % FBD
            st_y[ch][t, s * PART:(s + 1) * PART, :] = pan_y[ch][owner_row * FBD + inside]
            if ch == 0:
                tags = jnp.where(eight == inside, pay_y[owner_row, 8:16, :], 0).astype(F32)
                tag = jnp.sum(tags, axis=0, keepdims=True)
                for rep in range(8 // g.slot):
                    row = g.slot * PART + rep * g.slot + s
                    st_y[ch][t, row:row + 1, :] = tag
        if away:
            device = (me_r, col_of(x + dx, z + dz))
            remote(st_y[ch].at[t], gy_refs[ch].at[t], ex_s.at[0, ch], ex_r.at[0, ch], device).start()

    def send_z(ch, t, away):
        dr, dx = t // g.x, t % g.x
        to_row, from_x = (me_r + dr) % g.rows, (g.x - dx) % g.x
        first = smem_z[to_row, from_x, 0] // (FBD * g.cols)
        turn = (me_r - first + g.rows) % g.rows
        s, zz = turn % g.slot, turn // g.slot
        for j in range(g.pair):
            at = zz + g.span * j
            block = smem_z[to_row, from_x, s * g.cols + x * g.z + at]
            st_z[ch][t, j * PART:(j + 1) * PART, :] = pan_z[ch][at * FBD + block % FBD]
        if away:
            device = (to_row, col_of(x + dx, z))
            remote(st_z[ch].at[t], gz_refs[ch].at[t], ex_s.at[1, ch], ex_r.at[1, ch], device).start()

    ratio = g.n_z // g.n_y
    last = []
    for ch in range(CHUNKS):
        for j in range(1, ratio):
            send_z(ch, (j * 29) % g.n_z, True)

        @pl.loop(1, g.n_y)
        def _(q):
            send_y(ch, (q * 13) % g.n_y, True)
            for j in range(ratio):
                send_z(ch, ((ratio * q + j) * 29) % g.n_z, True)

        send_y(ch, 0, False)
        send_z(ch, 0, False)
        for which, (src, dst) in enumerate(((st_y, gy_refs), (st_z, gz_refs))):
            copy = pltpu.make_async_copy(src[ch].at[0], dst[ch].at[0], loc.at[base + 3 + 2 * ch + which])
            copy.start()
            last.append(copy)
        if ch + 1 < CHUNKS:
            gathers[ch + 1].advance(steps)
            gathers[ch + 1].finish()

    for copy in last:
        copy.wait()
    for dx in range(1, g.x):
        remote(tab.at[0], tab.at[dx], tab_s.at[dx - 1], tab_r.at[dx - 1], (me_r, col_of(x + dx, z))).wait_send()
    lists.drain()
    for gather in gathers:
        gather.drain()
    for ch in range(CHUNKS):
        for which, (src, dst, n) in enumerate(((st_y, gy_refs, g.n_y), (st_z, gz_refs, g.n_z))):
            view_s, view_d = src[ch].at[pl.ds(1, n - 1)], dst[ch].at[pl.ds(1, n - 1)]
            rest = remote(view_s, view_d, ex_s.at[which, ch], ex_r.at[which, ch], (me_r, col_of(x, z + 1)))
            rest.wait_send()
            rest.wait_recv()


def fetch(g, requests, cols, prolong_blocks):
    far_y, far_z = max(half_ring(g.y)), max(half_ring(g.z))
    dma = pltpu.SemaphoreType.DMA
    hbm = pl.BlockSpec(memory_space=pltpu.HBM)
    got = [jax.ShapeDtypeStruct((g.n_y, n, 128), F32) for n in g.out_y]
    got += [jax.ShapeDtypeStruct((g.n_z, n, 128), F32) for n in g.out_z]
    kinds = CHUNKS + 1
    return pl.pallas_call(
        functools.partial(fetch_kernel, g),
        out_shape=tuple(got),
        in_specs=[pl.BlockSpec(memory_space=pltpu.VMEM), hbm, hbm],
        out_specs=(hbm,) * (2 * CHUNKS),
        scratch_shapes=[
            *[pltpu.VMEM(s.shape, F32) for s in got],
            *[pltpu.VMEM((g.rows * FBD, PART, 128), F32) for _ in range(CHUNKS)],
            *[pltpu.VMEM((g.z * FBD, PART, 128), F32) for _ in range(CHUNKS)],
            pltpu.VMEM((g.rows, 16, 128), jnp.int32),
            pltpu.VMEM((g.z, 8, 128), jnp.int32),
            pltpu.VMEM((g.x, 1, 128), jnp.int32),
            pltpu.SMEM((g.z, 8, 128), jnp.int32),
            pltpu.SMEM((g.rows, 8, 128), jnp.int32),
            pltpu.SMEM(cols.shape, jnp.int32),
            dma((kinds, far_y)), dma((kinds, far_y)), dma((kinds, far_y)), dma((kinds, far_y)),
            dma((kinds, far_z)), dma((kinds, far_z)), dma((kinds, far_z)), dma((kinds, far_z)),
            dma((kinds, g.y)), dma((kinds, g.y)),
            dma((max(g.x - 1, 1),)), dma((max(g.x - 1, 1),)),
            dma((2, CHUNKS)), dma((2, CHUNKS)), dma((4 * CHUNKS + 3,)),
        ],
        compiler_params=pltpu.CompilerParams(
            collective_id=0, has_side_effects=True, vmem_limit_bytes=VMEM
        ),
        name="fetch",
    )(requests, cols, prolong_blocks)


def product_kernel(g, n_i, n_k, fetch_hbm, slot_hbm, count_hbm, rows_hbm, a_hbm, r_hbm, *refs):
    got_hbm, refs = refs[:2 * CHUNKS], refs[2 * CHUNKS:]
    acc_ref, got, refs = refs[0], refs[1:1 + 2 * CHUNKS], refs[1 + 2 * CHUNKS:]
    w, a_ref, r_ref, requests, slots, count, rows, tags, sem, a_sem = refs
    me_r, me_c = lax.axis_index("row"), lax.axis_index("col")
    x, z = me_c // g.z, me_c % g.z
    early = [
        pltpu.make_async_copy(rows_hbm, rows, sem.at[0]),
        pltpu.make_async_copy(count_hbm, count, sem.at[1]),
        pltpu.make_async_copy(r_hbm, r_ref, sem.at[2]),
    ]
    late = [
        pltpu.make_async_copy(slot_hbm, slots, sem.at[3]),
        pltpu.make_async_copy(fetch_hbm, requests, sem.at[4]),
        pltpu.make_async_copy(got_hbm[0].at[:, pl.ds(g.slot * PART, 8), :], tags, sem.at[5]),
    ]
    late += [pltpu.make_async_copy(src, dst, sem.at[6 + n]) for n, (src, dst) in enumerate(zip(got_hbm, got))]

    def block_row(i):
        return pltpu.make_async_copy(a_hbm.at[i], a_ref.at[i], a_sem.at[i])

    for copy in early:
        copy.start()
    for i in range(n_i):
        block_row(i).start()
    for copy in late:
        copy.start()
    acc_ref[...] = jnp.zeros_like(acc_ref)
    half = lax.broadcasted_iota(jnp.int32, (BS, 2 * BS), 1) // BS
    for copy in early:
        copy.wait()

    @pl.loop(0, n_i)
    def _(i):
        block_row(i).wait()
        stored = r_ref[i]
        swapped = pltpu.roll(stored, BS, 1)
        first, second = rows[0, i], rows[1, i]
        mine = jnp.where(half == 0, first, second)
        other = jnp.where(half == 0, second, first)
        dense = jnp.where(mine == half, stored, 0.0) + jnp.where(other == half, swapped, 0.0)
        r_hi, r_lo = split(dense)
        a_hi, a_lo = split(a_ref[i])
        ra = dot_t(
            jnp.concatenate([a_hi, a_lo, a_hi], axis=0),
            jnp.concatenate([r_hi, r_hi, r_lo], axis=0),
        )
        for k in range(n_k):
            part = jnp.where(k < count[i], ra[k * BS:(k + 1) * BS, :], 0.0)
            hi, lo = split(part)
            w[i * n_k + k, 0:BS, :] = hi
            w[i * n_k + k, BS:2 * BS, :] = lo

    for copy in late:
        copy.wait()

    @pl.loop(0, n_i)
    def _(i):
        for k in range(n_k):
            slot = slots[i, k]
            peer, s = slot // g.slot, slot % g.slot
            px, pz = peer // g.z, peer % g.z
            owner_row = requests[s, peer] // (FBD * g.cols)
            dx = (x - px + g.x) % g.x
            t = dx * g.z + (z - pz + g.z) % g.z
            tz = ((me_r - owner_row + g.rows) % g.rows) * g.x + dx
            j = pz // g.span
            top = [got[ch][t, pl.ds(pl.multiple_of(s * PART, 8), PART), :] for ch in range(CHUNKS)]
            bottom = [got[CHUNKS + ch][tz, pl.ds(pl.multiple_of(j * PART, 8), PART), :] for ch in range(CHUNKS)]
            p_hi, p_lo = split(jnp.concatenate(top + bottom, axis=0))
            w_hi, w_lo = w[i * n_k + k, 0:BS, :], w[i * n_k + k, BS:2 * BS, :]
            out = dot_t(jnp.concatenate([p_hi, p_lo, p_hi], axis=0), jnp.concatenate([w_hi, w_hi, w_lo], axis=0))
            first = tags[t, s, 0].astype(jnp.int32)
            second = tags[t, s, BS].astype(jnp.int32)
            acc_ref[first] += out[0:BS, :]
            acc_ref[second] += out[BS:2 * BS, :]


def product(g, requests, slots, counts, rows, blocks, restrict, got):
    n_i, n_k = slots.shape
    hbm = pl.BlockSpec(memory_space=pltpu.HBM)
    return pl.pallas_call(
        functools.partial(product_kernel, g, n_i, n_k),
        out_shape=jax.ShapeDtypeStruct((NCR * g.rows, BS, NCR * BS), F32),
        in_specs=[hbm] * (6 + 2 * CHUNKS),
        out_specs=pl.BlockSpec(memory_space=pltpu.VMEM),
        scratch_shapes=[
            *[pltpu.VMEM(a.shape, F32) for a in got],
            pltpu.VMEM((n_i * n_k, 2 * BS, NCR * BS), BF16),
            pltpu.VMEM(blocks.shape, F32),
            pltpu.VMEM(restrict.shape, F32),
            pltpu.SMEM(requests.shape, jnp.int32),
            pltpu.SMEM(slots.shape, jnp.int32),
            pltpu.SMEM(counts.shape, jnp.int32),
            pltpu.SMEM(rows.shape, jnp.int32),
            pltpu.SMEM((g.cols, 8, 128), F32),
            pltpu.SemaphoreType.DMA((6 + 2 * CHUNKS,)),
            pltpu.SemaphoreType.DMA((n_i,)),
        ],
        compiler_params=pltpu.CompilerParams(vmem_limit_bytes=VMEM),
        name="product",
    )(requests, slots, counts, rows, blocks, restrict, *got)


def reduce_kernel(g, acc_hbm, o_ref, acc, far, near, relay, relayed, s1, r2, sems, load, s2_send, s2_recv):
    me_r, me_c = lax.axis_index("row"), lax.axis_index("col")
    x, z = me_c // g.z, me_c % g.z
    half = BS // 2
    load_acc = pltpu.make_async_copy(acc_hbm, acc, load.at[0])
    load_acc.start()
    barrier = pltpu.get_barrier_semaphore()

    def at_x(dx):
        return (me_r, ((x + dx) % g.x) * g.z + z)

    def at_z(dz):
        return (me_r, x * g.z + (z + dz) % g.z)

    for device in [at_x(1), at_x(3)] + [at_z(dz) for dz in range(1, g.z)]:
        pl.semaphore_signal(barrier, inc=1, device_id=device, device_id_type=MESH)
    pl.semaphore_wait(barrier, g.z + 1)
    load_acc.wait()

    def tile(dx, dz):
        return ((x + dx) % g.x) * g.z + (z + dz) % g.z

    def send(kind, way, dz, src, dst):
        copy = pltpu.make_async_remote_copy(
            src_ref=src, dst_ref=dst.at[way, dz],
            send_sem=sems.at[kind, way, dz, 0], recv_sem=sems.at[kind, way, dz, 1],
            device_id=at_x(1 if way == 0 else 3), device_id_type=MESH,
        )
        copy.start()
        return copy

    order = sorted(range(g.z), key=lambda dz: -min(dz, g.z - dz))
    rows = (pl.ds(0, half), pl.ds(half, half))
    fars, nears, relays, lasts = {}, {}, {}, {}
    for dz in order:
        for way in range(2):
            fars[way, dz] = send(0, way, dz, acc.at[tile(2, dz), rows[way], :], far)
    for dz in order:
        for way in range(2):
            step = 1 if way == 0 else 3
            nears[way, dz] = send(1, way, dz, acc.at[tile(step, dz), rows[1 - way], :], near)
        for way in range(2):
            step = 1 if way == 0 else 3
            fars[way, dz].wait_recv()
            relay[way, dz] = acc[tile(step, dz), rows[way], :] + far[way, dz]
            relays[way, dz] = send(2, way, dz, relay.at[way, dz], relayed)
    for dz in order:
        for way in range(2):
            relays[way, dz].wait_recv()
            nears[1 - way, dz].wait_recv()
            s1[dz, rows[way], :] = acc[tile(0, dz), rows[way], :] + relayed[way, dz] + near[1 - way, dz]
        if dz:
            lasts[dz] = pltpu.make_async_remote_copy(
                src_ref=s1.at[dz], dst_ref=r2.at[dz - 1],
                send_sem=s2_send.at[dz - 1], recv_sem=s2_recv.at[dz - 1],
                device_id=at_z(dz), device_id_type=MESH,
            )
            lasts[dz].start()
    total = s1[0]
    for dz, copy in lasts.items():
        copy.wait_recv()
        total = total + r2[dz - 1]
    o_ref[...] = total
    for group in (fars, nears, relays, lasts):
        for copy in group.values():
            copy.wait_send()


def reduce(g, acc):
    rows, lanes = acc.shape[1:]
    part = pltpu.VMEM((2, g.z, rows // 2, lanes), F32)
    dma = pltpu.SemaphoreType.DMA
    return pl.pallas_call(
        functools.partial(reduce_kernel, g),
        out_shape=jax.ShapeDtypeStruct((rows, lanes), F32),
        in_specs=[pl.BlockSpec(memory_space=pltpu.HBM)],
        out_specs=pl.BlockSpec(memory_space=pltpu.VMEM),
        scratch_shapes=[
            pltpu.VMEM(acc.shape, F32),
            part, part, part, part,
            pltpu.VMEM((g.z, rows, lanes), F32),
            pltpu.VMEM((g.z - 1, rows, lanes), F32),
            dma((3, 2, g.z, 2)), dma((1,)), dma((g.z - 1,)), dma((g.z - 1,)),
        ],
        compiler_params=pltpu.CompilerParams(
            collective_id=1, has_side_effects=True, vmem_limit_bytes=VMEM
        ),
        name="reduce",
    )(acc)


def local(
    g,
    operator_blocks,
    operator_count,
    operator_slot,
    fetch_lists,
    prolong_blocks,
    prolong_cols,
    restrict_blocks,
    restrict_rows,
):
    requests = fetch_lists.reshape(g.cols, g.slot).T
    got = fetch(g, requests, prolong_cols.T, prolong_blocks)
    acc = product(
        g, requests, operator_slot, operator_count, restrict_rows.T, operator_blocks, restrict_blocks, got
    )
    share = reduce(g, acc)
    return share.T


def solution(mesh):
    g = Geometry(mesh.shape["row"], mesh.shape["col"])
    return jax.shard_map(
        functools.partial(local, g),
        mesh=mesh,
        in_specs=(
            P(("row", "col"), None, None),
            P(("row", "col")),
            P(("row", "col"), None),
            P("row", "col", None, None),
            P(("row", "col"), None, None),
            P(("row", "col"), None),
            P(("row", "col"), None, None),
            P(("row", "col"), None),
        ),
        out_specs=P("row", "col"),
        check_vma=False,
    )
```

```python
import functools

import jax
import jax.numpy as jnp
from jax import lax
from jax.experimental import pallas as pl
from jax.experimental.pallas import tpu as pltpu
from jax.sharding import PartitionSpec as P

MESH = pl.DeviceIdType.MESH
F32 = jnp.float32
BF16 = jnp.bfloat16

NX, NZ = 4, 8
CORES = 2
NCR = 2
FBD = 8
SLOT = 4
BS = 64
VMEM = 63 << 20
CHUNKS = 2
PART = BS // (2 * CHUNKS)


class Geometry:
    def __init__(self, rows, cols, x=NX, z=NZ, slot=SLOT):
        self.rows, self.cols, self.x, self.z, self.slot = rows, cols, x, z, slot
        self.y = rows // CORES
        self.span = rows // slot
        self.pair = z // self.span
        self.n_y, self.n_z = cols, rows * x
        self.out_y = [slot * PART for _ in range(CHUNKS)]
        self.out_z = [self.pair * PART for _ in range(CHUNKS)]


def half_ring(n):
    return n // 2, n - 1 - n // 2


def split(value):
    high = value.astype(BF16)
    return high, (value - high.astype(F32)).astype(BF16)


def dot_t(left, right):
    return lax.dot_general(left, right, (((0,), (0,)), ((), ())), preferred_element_type=F32)


class Ring:
    def __init__(self, steps, sign, send, recv, make):
        self.steps, self.sign, self.send, self.recv, self.make = steps, sign, send, recv, make

    def copy(self, t):
        return self.make(t, self.sign, self.send.at[t - 1], self.recv.at[t - 1])


def fetch_kernel(g, fl_ref, cols_hbm, p_hbm, gt_ref, *refs):
    gy_refs, gz_refs, st_y, st_z, pan_y, pan_z = (refs[n * CHUNKS:(n + 1) * CHUNKS] for n in range(6))
    (
        st_t, pay_y, pay_z, tab, smem_y, smem_z, cols,
        up_s, up_r, down_s, down_r, zup_s, zup_r, zdown_s, zdown_r, sib_s, sib_r, tab_s, tab_r, ex_s, ex_r, loc,
    ) = refs[6 * CHUNKS:]
    me_r, me_c = lax.axis_index("row"), lax.axis_index("col")
    y, core = me_r // CORES, me_r % CORES
    x, z = me_c // g.z, me_c % g.z

    def remote(src, dst, send, recv, device):
        return pltpu.make_async_remote_copy(
            src_ref=src, dst_ref=dst, send_sem=send, recv_sem=recv, device_id=device, device_id_type=MESH
        )

    def row_of(yy):
        return ((yy + g.y) % g.y) * CORES + core

    def col_of(xx, zz):
        return ((xx + g.x) % g.x) * g.z + (zz + g.z) % g.z

    own = []
    for ch in range(CHUNKS):
        top, bottom = ch * PART, (CHUNKS + ch) * PART
        own.append(pltpu.make_async_copy(
            p_hbm.at[:, pl.ds(top, PART), :], pan_y[ch].at[pl.ds(me_r * FBD, FBD)], loc.at[2 * ch]))
        own.append(pltpu.make_async_copy(
            p_hbm.at[:, pl.ds(bottom, PART), :], pan_z[ch].at[pl.ds(z * FBD, FBD)], loc.at[2 * ch + 1]))
    base = 2 * CHUNKS
    tag_in = pltpu.make_async_copy(cols_hbm, cols, loc.at[base])

    barrier = pltpu.get_barrier_semaphore()
    near = [(row_of(y + 1), me_c), (row_of(y - 1), me_c), (y * CORES + (1 - core), me_c)]
    near += [(me_r, col_of(x, z + 1)), (me_r, col_of(x, z - 1))]
    near += [(me_r, col_of(x + dx, z)) for dx in range(1, g.x)]
    for device in near:
        pl.semaphore_signal(barrier, inc=1, device_id=device, device_id_type=MESH)
    for copy in own + [tag_in]:
        copy.start()
    table = jnp.concatenate([fl_ref[s:s + 1, :] for s in range(g.slot)], axis=1)
    if table.shape[1] < 128:
        table = jnp.pad(table, ((0, 0), (0, 128 - table.shape[1])))
    tab[0] = table
    tag_in.wait()
    lane = lax.broadcasted_iota(jnp.int32, (1, 128), 1) // BS
    pay_y[me_r, 0:8, :] = jnp.zeros((8, 128), jnp.int32)
    pay_z[z] = jnp.zeros((8, 128), jnp.int32)
    for j in range(FBD):
        pay_y[me_r, 8 + j:9 + j, :] = jnp.where(lane == 0, cols[0, j], cols[1, j])
    for copy in own:
        copy.wait()
    pl.semaphore_wait(barrier, len(near))

    def rings_of(buf_y, buf_z, unit):
        def make_y(t, sign, send, recv):
            view = buf_y.at[pl.ds(row_of(y - sign * (t - 1)) * unit, unit)]
            return remote(view, view, send, recv, (row_of(y + sign), me_c))

        def make_z(t, sign, send, recv):
            view = buf_z.at[pl.ds((z - sign * (t - 1) + g.z) % g.z * unit, unit)]
            return remote(view, view, send, recv, (me_r, col_of(x, z + sign)))

        return make_y, make_z

    class Gather:
        def __init__(self, which, buf_y, buf_z, unit):
            make_y, make_z = rings_of(buf_y, buf_z, unit)
            (up_y, down_y), (up_z, down_z) = (half_ring(n)[::-1 if which % 2 else 1] for n in (g.y, g.z))
            self.y_rings = [
                Ring(up_y, 1, up_s.at[which], up_r.at[which], make_y),
                Ring(down_y, -1, down_s.at[which], down_r.at[which], make_y),
            ]
            self.z_rings = [
                Ring(up_z, 1, zup_s.at[which], zup_r.at[which], make_z),
                Ring(down_z, -1, zdown_s.at[which], zdown_r.at[which], make_z),
            ]
            self.rings = [self.y_rings[0], self.z_rings[0], self.y_rings[1], self.z_rings[1]]
            self.which, self.buf, self.unit, self.sibs = which, buf_y, unit, []

        def sibling(self, yy):
            n = len(self.sibs)
            view = self.buf.at[pl.ds(row_of(yy) * self.unit, self.unit)]
            copy = remote(
                view, view, sib_s.at[self.which, n], sib_r.at[self.which, n], (y * CORES + (1 - core), me_c))
            copy.start()
            self.sibs.append(copy)

        def begin(self):
            for ring in self.rings:
                if ring.steps:
                    ring.copy(1).start()
            self.sibling(y)

        def advance(self, t):
            for ring in self.rings:
                if t <= ring.steps:
                    ring.copy(t).wait_recv()
                    if t < ring.steps:
                        ring.copy(t + 1).start()
                    if ring in self.y_rings:
                        self.sibling(y - ring.sign * t)

        def finish(self):
            for copy in self.sibs:
                copy.wait_recv()

        def drain(self):
            for ring in self.rings:
                for t in range(1, ring.steps + 1):
                    ring.copy(t).wait_send()
            for copy in self.sibs:
                copy.wait_send()

    gathers = [Gather(ch, pan_y[ch], pan_z[ch], FBD) for ch in range(CHUNKS)]
    lists = Gather(CHUNKS, pay_y, pay_z, 1)
    steps = max(g.y, g.z) // 2

    for dx in range(1, g.x):
        remote(tab.at[0], tab.at[dx], tab_s.at[dx - 1], tab_r.at[dx - 1], (me_r, col_of(x + dx, z))).start()
    gathers[0].begin()
    for dx in range(g.x):
        if dx:
            remote(tab.at[0], tab.at[dx], tab_s.at[dx - 1], tab_r.at[dx - 1], (me_r, col_of(x + dx, z))).wait_recv()
        pay_y[me_r, dx:dx + 1, :] = tab[dx]
        pay_z[z, dx:dx + 1, :] = tab[dx]
    lists.begin()
    for ch in range(1, CHUNKS):
        gathers[ch].begin()
    to_smem = [
        pltpu.make_async_copy(pay_z, smem_y, loc.at[base + 1]),
        pltpu.make_async_copy(pay_y.at[:, 0:8, :], smem_z, loc.at[base + 2]),
    ]
    for t in range(1, steps + 1):
        lists.advance(t)
        if t == steps:
            lists.finish()
            for copy in to_smem:
                copy.start()
        gathers[0].advance(t)
        for ch in range(1, CHUNKS):
            if t < steps:
                gathers[ch].advance(t)
    gathers[0].finish()
    for copy in to_smem:
        copy.wait()

    eight = lax.broadcasted_iota(jnp.int32, (8, 128), 0)
    place = lax.broadcasted_iota(jnp.int32, (1, 128), 1) % BS // (BS // g.slot)

    def send_y(ch, t, away):
        dx, dz = t // g.z, t % g.z
        from_z, from_x = (z + dz) % g.z, (g.x - dx) % g.x
        row = jnp.zeros((1, 128), F32)
        for s in range(g.slot):
            block = smem_y[from_z, from_x, s * g.cols + me_c]
            owner_row, inside = block // (FBD * g.cols), block % FBD
            st_y[ch][t, s * PART:(s + 1) * PART, :] = pan_y[ch][owner_row * FBD + inside]
            if ch == 0:
                tags = jnp.where(eight == inside, pay_y[owner_row, 8:16, :], 0).astype(F32)
                row = jnp.where(place == s, jnp.sum(tags, axis=0, keepdims=True), row)
        if ch == 0:
            st_t[t] = row
        if away:
            device = (me_r, col_of(x + dx, z + dz))
            if ch == 0:
                remote(st_t.at[t], gt_ref.at[t], ex_s.at[2, 0], ex_r.at[2, 0], device).start()
            remote(st_y[ch].at[t], gy_refs[ch].at[t], ex_s.at[0, ch], ex_r.at[0, ch], device).start()

    def send_z(ch, t, away):
        dr, dx = t // g.x, t % g.x
        to_row, from_x = (me_r + dr) % g.rows, (g.x - dx) % g.x
        first = smem_z[to_row, from_x, 0] // (FBD * g.cols)
        turn = (me_r - first + g.rows) % g.rows
        s, zz = turn % g.slot, turn // g.slot
        for j in range(g.pair):
            at = zz + g.span * j
            block = smem_z[to_row, from_x, s * g.cols + x * g.z + at]
            st_z[ch][t, j * PART:(j + 1) * PART, :] = pan_z[ch][at * FBD + block % FBD]
        if away:
            device = (to_row, col_of(x + dx, z))
            remote(st_z[ch].at[t], gz_refs[ch].at[t], ex_s.at[1, ch], ex_r.at[1, ch], device).start()

    ratio = g.n_z // g.n_y
    last = []
    for ch in range(CHUNKS):
        for j in range(1, ratio):
            send_z(ch, (j * 29) % g.n_z, True)

        @pl.loop(1, g.n_y)
        def _(q):
            send_y(ch, (q * 13) % g.n_y, True)
            for j in range(ratio):
                send_z(ch, ((ratio * q + j) * 29) % g.n_z, True)

        send_y(ch, 0, False)
        send_z(ch, 0, False)
        for which, (src, dst) in enumerate(((st_y, gy_refs), (st_z, gz_refs))):
            copy = pltpu.make_async_copy(src[ch].at[0], dst[ch].at[0], loc.at[base + 3 + 2 * ch + which])
            copy.start()
            last.append(copy)
        if ch == 0:
            copy = pltpu.make_async_copy(st_t.at[0], gt_ref.at[0], loc.at[base + 3 + 2 * CHUNKS])
            copy.start()
            last.append(copy)
        if ch + 1 < CHUNKS:
            gathers[ch + 1].advance(steps)
            gathers[ch + 1].finish()

    for copy in last:
        copy.wait()
    for dx in range(1, g.x):
        remote(tab.at[0], tab.at[dx], tab_s.at[dx - 1], tab_r.at[dx - 1], (me_r, col_of(x + dx, z))).wait_send()
    lists.drain()
    for gather in gathers:
        gather.drain()
    view_s, view_d = st_t.at[pl.ds(1, g.n_y - 1)], gt_ref.at[pl.ds(1, g.n_y - 1)]
    rest = remote(view_s, view_d, ex_s.at[2, 0], ex_r.at[2, 0], (me_r, col_of(x, z + 1)))
    rest.wait_send()
    rest.wait_recv()
    for ch in range(CHUNKS):
        for which, (src, dst, n) in enumerate(((st_y, gy_refs, g.n_y), (st_z, gz_refs, g.n_z))):
            view_s, view_d = src[ch].at[pl.ds(1, n - 1)], dst[ch].at[pl.ds(1, n - 1)]
            rest = remote(view_s, view_d, ex_s.at[which, ch], ex_r.at[which, ch], (me_r, col_of(x, z + 1)))
            rest.wait_send()
            rest.wait_recv()


def fetch(g, requests, cols, prolong_blocks):
    far_y, far_z = max(half_ring(g.y)), max(half_ring(g.z))
    dma = pltpu.SemaphoreType.DMA
    hbm = pl.BlockSpec(memory_space=pltpu.HBM)
    got = [jax.ShapeDtypeStruct((g.n_y, n, 128), F32) for n in g.out_y]
    got += [jax.ShapeDtypeStruct((g.n_z, n, 128), F32) for n in g.out_z]
    kinds = CHUNKS + 1
    return pl.pallas_call(
        functools.partial(fetch_kernel, g),
        out_shape=(jax.ShapeDtypeStruct((g.n_y, 1, 128), F32), *got),
        in_specs=[pl.BlockSpec(memory_space=pltpu.VMEM), hbm, hbm],
        out_specs=(hbm,) * (2 * CHUNKS + 1),
        scratch_shapes=[
            *[pltpu.VMEM(s.shape, F32) for s in got],
            *[pltpu.VMEM((g.rows * FBD, PART, 128), F32) for _ in range(CHUNKS)],
            *[pltpu.VMEM((g.z * FBD, PART, 128), F32) for _ in range(CHUNKS)],
            pltpu.VMEM((g.n_y, 1, 128), F32),
            pltpu.VMEM((g.rows, 16, 128), jnp.int32),
            pltpu.VMEM((g.z, 8, 128), jnp.int32),
            pltpu.VMEM((g.x, 1, 128), jnp.int32),
            pltpu.SMEM((g.z, 8, 128), jnp.int32),
            pltpu.SMEM((g.rows, 8, 128), jnp.int32),
            pltpu.SMEM(cols.shape, jnp.int32),
            dma((kinds, far_y)), dma((kinds, far_y)), dma((kinds, far_y)), dma((kinds, far_y)),
            dma((kinds, far_z)), dma((kinds, far_z)), dma((kinds, far_z)), dma((kinds, far_z)),
            dma((kinds, g.y)), dma((kinds, g.y)),
            dma((max(g.x - 1, 1),)), dma((max(g.x - 1, 1),)),
            dma((3, CHUNKS)), dma((3, CHUNKS)), dma((4 * CHUNKS + 4,)),
        ],
        compiler_params=pltpu.CompilerParams(
            collective_id=0, has_side_effects=True, vmem_limit_bytes=VMEM
        ),
        name="fetch",
    )(requests, cols, prolong_blocks)


def product_kernel(g, n_i, n_k, fetch_hbm, slot_hbm, count_hbm, rows_hbm, a_hbm, r_hbm, tag_hbm, *refs):
    got_hbm, refs = refs[:2 * CHUNKS], refs[2 * CHUNKS:]
    acc_ref, got, refs = refs[0], refs[1:1 + 2 * CHUNKS], refs[1 + 2 * CHUNKS:]
    w, a_ref, r_ref, requests, slots, count, rows, tags, sem, a_sem = refs
    me_r, me_c = lax.axis_index("row"), lax.axis_index("col")
    x, z = me_c // g.z, me_c % g.z
    early = [
        pltpu.make_async_copy(rows_hbm, rows, sem.at[0]),
        pltpu.make_async_copy(count_hbm, count, sem.at[1]),
        pltpu.make_async_copy(r_hbm, r_ref, sem.at[2]),
    ]
    late = [
        pltpu.make_async_copy(slot_hbm, slots, sem.at[3]),
        pltpu.make_async_copy(fetch_hbm, requests, sem.at[4]),
        pltpu.make_async_copy(tag_hbm, tags, sem.at[5]),
    ]
    late += [pltpu.make_async_copy(src, dst, sem.at[6 + n]) for n, (src, dst) in enumerate(zip(got_hbm, got))]

    def block_row(i):
        return pltpu.make_async_copy(a_hbm.at[i], a_ref.at[i], a_sem.at[i])

    for copy in early:
        copy.start()
    for i in range(n_i):
        block_row(i).start()
    for copy in late:
        copy.start()
    acc_ref[...] = jnp.zeros_like(acc_ref)
    half = lax.broadcasted_iota(jnp.int32, (BS, 2 * BS), 1) // BS
    for copy in early:
        copy.wait()

    @pl.loop(0, n_i)
    def _(i):
        block_row(i).wait()
        stored = r_ref[i]
        swapped = pltpu.roll(stored, BS, 1)
        first, second = rows[0, i], rows[1, i]
        mine = jnp.where(half == 0, first, second)
        other = jnp.where(half == 0, second, first)
        dense = jnp.where(mine == half, stored, 0.0) + jnp.where(other == half, swapped, 0.0)
        r_hi, r_lo = split(dense)
        a_hi, a_lo = split(a_ref[i])
        ra = dot_t(
            jnp.concatenate([a_hi, a_lo, a_hi], axis=0),
            jnp.concatenate([r_hi, r_hi, r_lo], axis=0),
        )
        for k in range(n_k):
            part = jnp.where(k < count[i], ra[k * BS:(k + 1) * BS, :], 0.0)
            hi, lo = split(part)
            w[i * n_k + k, 0:BS, :] = hi
            w[i * n_k + k, BS:2 * BS, :] = lo

    for copy in late:
        copy.wait()

    @pl.loop(0, n_i)
    def _(i):
        for k in range(n_k):
            slot = slots[i, k]
            peer, s = slot // g.slot, slot % g.slot
            px, pz = peer // g.z, peer % g.z
            owner_row = requests[s, peer] // (FBD * g.cols)
            dx = (x - px + g.x) % g.x
            t = dx * g.z + (z - pz + g.z) % g.z
            tz = ((me_r - owner_row + g.rows) % g.rows) * g.x + dx
            j = pz // g.span
            top = [got[ch][t, pl.ds(pl.multiple_of(s * PART, 8), PART), :] for ch in range(CHUNKS)]
            bottom = [got[CHUNKS + ch][tz, pl.ds(pl.multiple_of(j * PART, 8), PART), :] for ch in range(CHUNKS)]
            p_hi, p_lo = split(jnp.concatenate(top + bottom, axis=0))
            w_hi, w_lo = w[i * n_k + k, 0:BS, :], w[i * n_k + k, BS:2 * BS, :]
            out = dot_t(jnp.concatenate([p_hi, p_lo, p_hi], axis=0), jnp.concatenate([w_hi, w_hi, w_lo], axis=0))
            first = tags[t, 0, s * (BS // g.slot)].astype(jnp.int32)
            second = tags[t, 0, BS + s * (BS // g.slot)].astype(jnp.int32)
            acc_ref[first] += out[0:BS, :]
            acc_ref[second] += out[BS:2 * BS, :]


def product(g, requests, slots, counts, rows, blocks, restrict, tags, got):
    n_i, n_k = slots.shape
    hbm = pl.BlockSpec(memory_space=pltpu.HBM)
    return pl.pallas_call(
        functools.partial(product_kernel, g, n_i, n_k),
        out_shape=jax.ShapeDtypeStruct((NCR * g.rows, BS, NCR * BS), F32),
        in_specs=[hbm] * (7 + 2 * CHUNKS),
        out_specs=pl.BlockSpec(memory_space=pltpu.VMEM),
        scratch_shapes=[
            *[pltpu.VMEM(a.shape, F32) for a in got],
            pltpu.VMEM((n_i * n_k, 2 * BS, NCR * BS), BF16),
            pltpu.VMEM(blocks.shape, F32),
            pltpu.VMEM(restrict.shape, F32),
            pltpu.SMEM(requests.shape, jnp.int32),
            pltpu.SMEM(slots.shape, jnp.int32),
            pltpu.SMEM(counts.shape, jnp.int32),
            pltpu.SMEM(rows.shape, jnp.int32),
            pltpu.SMEM(tags.shape, F32),
            pltpu.SemaphoreType.DMA((6 + 2 * CHUNKS,)),
            pltpu.SemaphoreType.DMA((n_i,)),
        ],
        compiler_params=pltpu.CompilerParams(vmem_limit_bytes=VMEM),
        name="product",
    )(requests, slots, counts, rows, blocks, restrict, tags, *got)


def reduce_kernel(g, acc_hbm, o_ref, acc, far, near, relay, relayed, s1, r2, sems, load, s2_send, s2_recv):
    me_r, me_c = lax.axis_index("row"), lax.axis_index("col")
    x, z = me_c // g.z, me_c % g.z
    half = BS // 2
    load_acc = pltpu.make_async_copy(acc_hbm, acc, load.at[0])
    load_acc.start()
    barrier = pltpu.get_barrier_semaphore()

    def at_x(dx):
        return (me_r, ((x + dx) % g.x) * g.z + z)

    def at_z(dz):
        return (me_r, x * g.z + (z + dz) % g.z)

    for device in [at_x(1), at_x(3)] + [at_z(dz) for dz in range(1, g.z)]:
        pl.semaphore_signal(barrier, inc=1, device_id=device, device_id_type=MESH)
    pl.semaphore_wait(barrier, g.z + 1)
    load_acc.wait()

    def tile(dx, dz):
        return ((x + dx) % g.x) * g.z + (z + dz) % g.z

    def send(kind, way, dz, src, dst):
        copy = pltpu.make_async_remote_copy(
            src_ref=src, dst_ref=dst.at[way, dz],
            send_sem=sems.at[kind, way, dz, 0], recv_sem=sems.at[kind, way, dz, 1],
            device_id=at_x(1 if way == 0 else 3), device_id_type=MESH,
        )
        copy.start()
        return copy

    order = sorted(range(g.z), key=lambda dz: -min(dz, g.z - dz))
    rows = (pl.ds(0, half), pl.ds(half, half))
    fars, nears, relays, lasts = {}, {}, {}, {}
    for dz in order:
        for way in range(2):
            fars[way, dz] = send(0, way, dz, acc.at[tile(2, dz), rows[way], :], far)
    for dz in order:
        for way in range(2):
            step = 1 if way == 0 else 3
            nears[way, dz] = send(1, way, dz, acc.at[tile(step, dz), rows[1 - way], :], near)
        for way in range(2):
            step = 1 if way == 0 else 3
            fars[way, dz].wait_recv()
            relay[way, dz] = acc[tile(step, dz), rows[way], :] + far[way, dz]
            relays[way, dz] = send(2, way, dz, relay.at[way, dz], relayed)
    for dz in order:
        for way in range(2):
            relays[way, dz].wait_recv()
            nears[1 - way, dz].wait_recv()
            s1[dz, rows[way], :] = acc[tile(0, dz), rows[way], :] + relayed[way, dz] + near[1 - way, dz]
        if dz:
            lasts[dz] = pltpu.make_async_remote_copy(
                src_ref=s1.at[dz], dst_ref=r2.at[dz - 1],
                send_sem=s2_send.at[dz - 1], recv_sem=s2_recv.at[dz - 1],
                device_id=at_z(dz), device_id_type=MESH,
            )
            lasts[dz].start()
    total = s1[0]
    for dz, copy in lasts.items():
        copy.wait_recv()
        total = total + r2[dz - 1]
    o_ref[...] = total
    for group in (fars, nears, relays, lasts):
        for copy in group.values():
            copy.wait_send()


def reduce(g, acc):
    rows, lanes = acc.shape[1:]
    part = pltpu.VMEM((2, g.z, rows // 2, lanes), F32)
    dma = pltpu.SemaphoreType.DMA
    return pl.pallas_call(
        functools.partial(reduce_kernel, g),
        out_shape=jax.ShapeDtypeStruct((rows, lanes), F32),
        in_specs=[pl.BlockSpec(memory_space=pltpu.HBM)],
        out_specs=pl.BlockSpec(memory_space=pltpu.VMEM),
        scratch_shapes=[
            pltpu.VMEM(acc.shape, F32),
            part, part, part, part,
            pltpu.VMEM((g.z, rows, lanes), F32),
            pltpu.VMEM((g.z - 1, rows, lanes), F32),
            dma((3, 2, g.z, 2)), dma((1,)), dma((g.z - 1,)), dma((g.z - 1,)),
        ],
        compiler_params=pltpu.CompilerParams(
            collective_id=1, has_side_effects=True, vmem_limit_bytes=VMEM
        ),
        name="reduce",
    )(acc)


def local(
    g,
    operator_blocks,
    operator_count,
    operator_slot,
    fetch_lists,
    prolong_blocks,
    prolong_cols,
    restrict_blocks,
    restrict_rows,
):
    requests = fetch_lists.reshape(g.cols, g.slot).T
    tags, *got = fetch(g, requests, prolong_cols.T, prolong_blocks)
    acc = product(
        g, requests, operator_slot, operator_count, restrict_rows.T, operator_blocks, restrict_blocks, tags, got
    )
    share = reduce(g, acc)
    return share.T


def solution(mesh):
    g = Geometry(mesh.shape["row"], mesh.shape["col"])
    return jax.shard_map(
        functools.partial(local, g),
        mesh=mesh,
        in_specs=(
            P(("row", "col"), None, None),
            P(("row", "col")),
            P(("row", "col"), None),
            P("row", "col", None, None),
            P(("row", "col"), None, None),
            P(("row", "col"), None),
            P(("row", "col"), None, None),
            P(("row", "col"), None),
        ),
        out_specs=P("row", "col"),
        check_vma=False,
    )
```
